128 devices in a mesh: bin: 4 (over y), grp: 32 (over x, z, core).
Axes of the slice: x: 4, y: 4, z: 4, core: 2. Of those that a mesh axis runs over, the one named last changes fastest.
Arguments:
- templates: bfloat16 [131072, 512], P(('bin', 'grp')), may hold values from -6 to 6
- owner_device: int32 [131072, 1], P(('bin', 'grp')), may hold values from 0 to 127; in each aligned block of 1024 rows (0 to 1023, 1024 to 2047, ...) at most 16 rows name the same one
- rate_code: int32 [131072], P(('bin', 'grp')), may hold values from 0 to 4
- rate_gains: float32 [5, 512], replicated, may hold values from 0.5 to 2
- sketch: float32 [512, 256], replicated, may hold values from -6 to 6
- strain: float32 [2, 262144], P(None, 'grp'), may hold values from -6 to 6
Outputs:
- mixing: bfloat16 [131072, 256], P(('bin', 'grp'))
- spectrum: float32 [4, 256], P('bin')
- filtered_0: bfloat16 [4, 2, 262144, 256], P('bin', None, 'grp')
- filtered_1: bfloat16 [4, 2, 131072, 256], P('bin', None, 'grp')
- filtered_2: bfloat16 [4, 2, 65536, 256], P('bin', None, 'grp')
- filtered_3: bfloat16 [4, 2, 32768, 256], P('bin', None, 'grp')
- filtered_4: bfloat16 [4, 2, 16384, 256], P('bin', None, 'grp')
The draws below stay inside these ranges and needn't reach their ends.
Inputs may be any that keep to these rules, and one draw needn't show every extreme that they name: `owner_device`: among the rows of one device, no device is named by more than 16 rows, and some device is named by exactly 16 rows.
All inputs are finite; a program needn't handle non-finite values.
Results may differ from the reference program's by a relative error of at most 0.0059.
Values may be sent and summed in bfloat16 or wider, within the bound.
A program may use at most 128 MiB of HBM per device.

```python
import math
import jax
import jax.numpy as jnp
import numpy as np
from jax import lax

L = 512
K = 256
RATES = 5
DETECTORS = 2
TPL_DEV = 1024
TEMPLATES = 131072
CAP = 16
BINS = 4
BIN_ROWS = 32768
SAMPLES = 262144
N_GRP = 32
DEVICES = 128


def set_ends(array, rng, smallest, top_value):
    spot = [jax.random.randint(jax.random.fold_in(rng, axis), (), 0, length) for axis, length in enumerate(array.shape)]
    longest = array.shape.index(max(array.shape))
    next_to = spot[:longest] + [(spot[longest] + 1) % array.shape[longest]] + spot[longest + 1:]
    return array.at[tuple(spot)].set(smallest).at[tuple(next_to)].set(top_value)


def shard_levels(own_key, extent, split, least, high):
    factor_of = 1.0
    for axis_at, blocks in split:
        heights = jax.random.uniform(jax.random.fold_in(jax.random.fold_in(own_key, 6), axis_at), (blocks,), jnp.float32, least / len(split), high / len(split))
        factor_of = factor_of * jnp.repeat(jnp.exp(heights), extent[axis_at] // blocks).reshape((-1,) + (1,) * (len(extent) - 1 - axis_at))
    return factor_of


def assign_block(rng, own, number, rows, count, top, reach, lean):
    ranking = jax.random.permutation(rng, count)
    heavy_load, ordinary = shares(count, rows * top, reach, lean, True), shares(count, rows * top, reach, lean, False)
    places = jnp.arange(count)

    def named(tallies, rotation):
        used = int((tallies > 0).sum())
        fixed = max(1, used // 4)
        shifted = fixed + (places - fixed + rotation * (used - fixed)) % max(1, count - fixed)
        return jnp.zeros((count,), jnp.int32).at[ranking[jnp.where(places < fixed, places, shifted)]].set(jnp.asarray(tallies, jnp.int32))

    tallies = jnp.where(number % 4 == 0, named(heavy_load, number // 4), named(ordinary, number - number // 4 - 1))
    mixed = jax.random.permutation(jax.random.fold_in(own, 3), count)
    source_of, receiver = mixed[0:count // 2 * 2:2], mixed[1:count // 2 * 2:2]
    margin = jnp.minimum(tallies[source_of] - 1, reach - tallies[receiver]) // 2
    margin = jnp.where((source_of == ranking[0]) | (receiver == ranking[0]) | (tallies[receiver] == 0), 0, jnp.maximum(margin, 0))
    shifted = jax.random.randint(jax.random.fold_in(own, 4), (count // 2,), 0, 1 << 20) % (margin + 1)
    tallies = tallies.at[source_of].add(-shifted).at[receiver].add(shifted)
    items = jnp.searchsorted(jnp.cumsum(tallies), jnp.arange(rows * top), side="right").astype(jnp.int32)
    table = items.reshape(top, rows).T
    table = table[jax.random.permutation(jax.random.fold_in(own, 1), rows)]
    rotation = jax.random.randint(jax.random.fold_in(own, 2), (rows, 1), 0, top)
    return jnp.take_along_axis(table, (jnp.arange(top)[None, :] + rotation) % top, axis=1)


def shares(count, total, most, slope, full):
    loads = [(1 << 20) // math.isqrt(grade ** slope) + 1 for grade in range(1, count + 1)]
    largest = most if full else min(most, max(-(-total // count), total * loads[0] // sum(loads)))
    least = 1 if total - largest >= count - 1 else 0
    holding, spare = [largest] + [least] * (count - 1), total - largest - least * (count - 1)
    while spare > 0:
        movable = [i for i in range(1, count) if holding[i] < largest] or [i for i in range(1, count) if holding[i] < most]
        mass, remaining = sum([loads[i] for i in movable]), spare
        for i in movable:
            more = min(most - holding[i], max(1, remaining * loads[i] // mass), spare)
            holding[i] = holding[i] + more
            spare = spare - more
    return np.array(holding)


def scatter_about(rng, shape, width, most, cuts=(), kind=jnp.bfloat16):
    result = width * jax.random.normal(rng, shape, jnp.float32)
    if cuts:
        result = result * shard_levels(rng, shape, cuts, -0.22, 0.18)
    return jnp.clip(result, -most, most).astype(kind)


def setup_inputs(seed: int = 0) -> dict:
    splits = jax.random.split(jax.random.key(seed), 7)
    templates = scatter_about(splits[0], (TEMPLATES, L), 1.0, 6.0, ((0, 128),))
    owner_device_keys = jax.random.split(jax.random.fold_in(splits[1], 1), TEMPLATES // TPL_DEV)
    owner_device_turns = jax.random.permutation(jax.random.fold_in(splits[1], 3), TEMPLATES // TPL_DEV)
    owner_device = jax.vmap(lambda own, number: assign_block(jax.random.fold_in(splits[1], 2), own, number, TPL_DEV, DEVICES, 1, CAP, 2))(owner_device_keys, owner_device_turns).reshape((TEMPLATES, 1))
    rate_code = set_ends(jax.random.randint(splits[2], (TEMPLATES,), 0, RATES), jax.random.fold_in(splits[2], 1), 0, RATES - 1).astype(jnp.int32)
    rate_gains = jnp.clip(jnp.exp(jax.random.uniform(splits[3], (RATES, L), jnp.float32, math.log(0.5), math.log(2.0))), 0.5, 2.0)
    sketch = scatter_about(splits[4], (L, K), 1.0, 6.0, (), jnp.float32)
    strain = scatter_about(splits[5], (DETECTORS, SAMPLES), 1.0, 6.0, ((1, 32),), jnp.float32)
    return dict(templates=templates, owner_device=owner_device, rate_code=rate_code, rate_gains=rate_gains, sketch=sketch, strain=strain)


highest = lax.Precision.HIGHEST
inv_root_two = 0.7071067811865476

def whiten_rows(templates, rate_code, rate_gains):
    factor = jnp.zeros(templates.shape, jnp.float32)
    for rate_level in range(rate_gains.shape[0]):
        factor = factor + jnp.where((rate_code == rate_level)[:, None], rate_gains[rate_level][None, :], jnp.float32(0.0))
    return (templates.astype(jnp.float32) * factor).astype(jnp.bfloat16)

def reference(templates, owner_device, rate_code, rate_gains, sketch, strain):
    whitened = whiten_rows(templates, rate_code, rate_gains)
    wide_rows = whitened.astype(jnp.float32)
    bin_of_row = owner_device[:, 0] // N_GRP
    spectra = []
    bases = []
    mixing = jnp.zeros((wide_rows.shape[0], K), jnp.float32)
    for bin_number in range(BINS):
        member = bin_of_row == bin_number
        masked = jnp.where(member[:, None], wide_rows, jnp.float32(0.0))
        gram_total = lax.dot_general(masked, wide_rows, (((0,), (0,)), ((), ())), precision=highest)
        product = jnp.dot(gram_total, sketch, precision=highest)
        inner_gram = jnp.dot(product.T, product, precision=highest)
        lower_factor = jnp.linalg.cholesky(inner_gram)
        spectra.append(jnp.diagonal(lower_factor) / (BIN_ROWS * math.sqrt(L)))
        basis_bf = jax.scipy.linalg.solve_triangular(lower_factor, product.T, lower=True).T.astype(jnp.bfloat16)
        bases.append(basis_bf)
        coeffs = jnp.dot(wide_rows, basis_bf.astype(jnp.float32), precision=highest)
        mixing = mixing + jnp.where(member[:, None], coeffs, jnp.float32(0.0))
    outputs = [mixing.astype(jnp.bfloat16), jnp.stack(spectra)]
    current = strain
    for rate_level in range(RATES):
        if rate_level > 0:
            paired = current.reshape(current.shape[0], -1, 2)
            current = (paired[:, :, 0] + paired[:, :, 1]) * inv_root_two
        rounded = lax.optimization_barrier(current.astype(jnp.bfloat16)).astype(jnp.float32)
        stride = 2 ** rate_level
        per_bin = []
        for bin_number in range(BINS):
            tap_rows = bases[bin_number][::stride].astype(jnp.float32)
            tap_count = tap_rows.shape[0]
            result_level = lax.conv_general_dilated(rounded[:, :, None], tap_rows[::-1][:, None, :], (1,), [(tap_count - 1, 0)], dimension_numbers=('NWC', 'WIO', 'NWC'), precision=highest)
            per_bin.append(result_level.astype(jnp.bfloat16))
        outputs.append(jnp.stack(per_bin))
    return (outputs[0], outputs[1], outputs[2], outputs[3], outputs[4], outputs[5], outputs[6])
```

```python
import functools
import math

import jax
import jax.numpy as jnp
from jax import lax
from jax.experimental import pallas as pl
from jax.experimental.pallas import tpu as pltpu
from jax.sharding import PartitionSpec as P

f32, bf16 = jnp.float32, jnp.bfloat16
highest = lax.Precision.HIGHEST
inv_root_two = 0.7071067811865476
LANES = 128
VMEM_LIMIT = 56 << 20


def dot(a, b, ca, cb, precision=None):
    return lax.dot_general(
        a, b, (((ca,), (cb,)), ((), ())), precision=precision, preferred_element_type=f32
    )


def split(x, parts):
    out = []
    for _ in range(parts):
        piece = x.astype(bf16)
        out.append(piece)
        x = x - piece.astype(f32)
    return out


def partial_kernel(bins, t_ref, code_ref, gains_ref, sketch_ref, white_ref, part_ref):
    rows, length = t_ref.shape
    width = sketch_ref.shape[1]
    code = code_ref[...]
    rate = jnp.broadcast_to(code % 8, (24, rows))
    which = lax.broadcasted_iota(jnp.int32, (24, rows), 0) % 8
    onehot = jnp.where(rate == which, 1.0, 0.0).astype(bf16)
    gains = gains_ref[...]
    gains = jnp.concatenate(split(gains, 3), axis=0)
    factor = dot(onehot, gains, 0, 0)
    white = (t_ref[...].astype(f32) * factor).astype(bf16)
    white_ref[...] = white
    sk = split(sketch_ref[...], 2)
    y = dot(white, sk[0], 1, 0) + dot(white, sk[1], 1, 0)
    bin_col = jnp.transpose(jnp.broadcast_to(code // 8, (8, rows)).astype(f32))[:, 0:1]
    yh, yl = split(y, 2)
    yh, yl = yh.astype(f32), yl.astype(f32)
    for b in range(bins):
        m = bin_col == float(b)
        yb = jnp.concatenate(
            [jnp.where(m, yh, 0.0).astype(bf16), jnp.where(m, yl, 0.0).astype(bf16)], axis=1
        )
        pb = dot(white, yb, 0, 0)
        part_ref[b] = pb[:, :width] + pb[:, width:]


def eliminate(D, nb, w=8):
    groups = nb // 8
    W2 = 2 * nb
    ri = lax.broadcasted_iota(jnp.int32, (nb, nb), 0)
    ci = lax.broadcasted_iota(jnp.int32, (nb, nb), 1)
    eye = jnp.where(ri == ci, 1.0, 0.0).astype(f32)
    M = jnp.concatenate([D, eye], axis=1)
    Mv = [M[8 * k : 8 * k + 8, :] for k in range(groups)]
    sub = lax.broadcasted_iota(jnp.int32, (8, W2), 0)
    spread = lambda x: jnp.broadcast_to(x, (8, W2))
    for j in range(0, nb, w):
        g = j // 8
        a = [spread(Mv[(j + s) // 8][(j + s) % 8 : (j + s) % 8 + 1, :]) for s in range(w)]
        S = [
            [spread(a[s][:, j + t : j + t + 1]) if t >= s else None for t in range(w)]
            for s in range(w)
        ]
        c = {k: [spread(Mv[k][:, j + s : j + s + 1]) for s in range(w)] for k in range(g, groups)}
        inv = []
        for s in range(w):
            iv = 1.0 / S[s][s]
            inv.append(iv)
            for t in range(s + 1, w):
                f = S[s][t] * iv
                for u in range(t, w):
                    S[t][u] = S[t][u] - f * S[s][u]
                a[t] = a[t] - f * a[s]
        for k in range(g, groups):
            acc = Mv[k]
            for s in range(w):
                m = c[k][s] * inv[s]
                if k * 8 <= j + s:
                    m = jnp.where(sub + 8 * k > j + s, m, 0.0)
                acc = acc - m * a[s]
                for t in range(s + 1, w):
                    c[k][t] = c[k][t] - m * S[s][t]
            Mv[k] = acc
    M = jnp.concatenate(Mv, axis=0)
    diag = jnp.where(ri == ci, M[:, :nb], 0.0)
    d_col = jnp.sum(diag, axis=1, keepdims=True)
    d_row = jnp.sum(diag, axis=0, keepdims=True)
    return M[:, nb:] * lax.rsqrt(d_col), d_row * lax.rsqrt(d_row)


def basis_steps(product, scale, A, X, spec_ref):
    n, nb = product.shape[1], 128
    A[...] = dot(product, product, 0, 0, highest)
    X0, d0 = eliminate(A[:nb, :nb], nb)
    R = dot(X0, A[:nb, nb:], 1, 0, highest)
    X1, d1 = eliminate(A[nb:, nb:] - dot(R, R, 0, 0, highest), nb)
    X[:nb, :nb] = X0
    X[:nb, nb:] = jnp.zeros((nb, n - nb), f32)
    X[nb:, nb:] = X1
    X[nb:, :nb] = -dot(X1, dot(R, X0, 0, 0, highest), 1, 0, highest)
    spec_ref[...] = jnp.concatenate([d0, d1], axis=1) * scale
    return dot(product, X[...], 1, 1, highest).astype(bf16)


def basis_kernel(scale, p_ref, basis_ref, spec_ref, A, X):
    basis_ref[...] = basis_steps(p_ref[...], scale, A, X, spec_ref)


def filter_kernel(lead, xe_ref, basis_ref, *rest):
    outs, (rv0, rv1, rv2, rv3, rv4, bwide, strip), (o0, o1, o2, o3, o4), sems = (
        rest[:5], rest[5:12], rest[12:17], rest[17]
    )
    rvs, obufs = (rv0, rv1, rv2, rv3, rv4), (o0, o1, o2, o3, o4)
    levels = len(outs)
    n = LANES
    ri = lax.broadcasted_iota(jnp.int32, (n, n), 0)
    ci = lax.broadcasted_iota(jnp.int32, (n, n), 1)
    flip = jnp.where(ri + ci == n - 1, 1.0, 0.0).astype(f32)
    first = jnp.where(ri // 2 == ci, 1.0, 0.0).astype(f32)
    second = jnp.where(ri // 2 == ci - n // 2, 1.0, 0.0).astype(f32)
    rv0[...] = dot(xe_ref[...], flip, 1, 0, highest)
    for r in range(1, levels):
        count = rvs[r].shape[0]
        later = rvs[r - 1][pl.ds(1, count, stride=2), :]
        earlier = rvs[r - 1][pl.ds(0, count, stride=2), :]
        rvs[r][...] = (
            dot(later, first, 1, 0, highest) + dot(earlier, second, 1, 0, highest)
        ) * inv_root_two
    for h in range(bwide.shape[0]):
        bwide[h] = basis_ref[:, h * n : (h + 1) * n].astype(f32)

    def every(taps, step):
        halves = [bwide[h, pl.ds(0, taps, stride=step), :] for h in range(bwide.shape[0])]
        return jnp.concatenate(halves, axis=1)

    length, width = basis_ref.shape
    base = 0
    copies = []
    for r in range(levels):
        taps = length >> r
        blocks = max(1, taps // n)
        rows = rvs[r].shape[0] // 2
        head = lead >> r
        tiles = rows - head
        held = tiles + blocks - 1
        if taps >= n:
            weight = every(taps, 1 << r).astype(bf16) if r else basis_ref[...]
        else:
            weight = jnp.concatenate(
                [every(taps, 1 << r), jnp.zeros((n - taps, width), f32)], axis=0
            ).astype(bf16)
        bwide_r = weight
        group = min(8, tiles)
        for d in range(2):
            first_col = base

            def build(p, carry, r=r, d=d, rows=rows, first_col=first_col):
                q = d * rows + rows - 1 - p
                z = jnp.concatenate(
                    [rvs[r][pl.ds(q, 1), :], rvs[r][pl.ds(q - 1, 1), :]], axis=1
                ).astype(bf16).astype(f32)
                z = jnp.broadcast_to(z, (n, 2 * n))
                t = pltpu.roll(z, n + 1, 1, stride=1, stride_axis=0)[:, :n]
                strip[:, pl.ds(pl.multiple_of((first_col + p) * n, n), n)] = t.astype(bf16)
                return carry

            lax.fori_loop(0, held, build, 0)

            def tile(s, carry, r=r, d=d, rows=rows, first_col=first_col, group=group,
                     blocks=blocks, weight=bwide_r, tiles=tiles):
                parts = []
                for i in range(group):
                    p = first_col + tiles - 1 - (s * group + i)
                    parts.append(strip[:, pl.ds(pl.multiple_of(p * n, n), blocks * n)])
                lhs = jnp.concatenate(parts, axis=0)
                span = group * n
                obufs[r][d, pl.ds(pl.multiple_of(s * span, span), span), :] = dot(
                    lhs, weight, 1, 0
                ).astype(bf16)
                pltpu.make_async_copy(
                    obufs[r].at[d, pl.ds(pl.multiple_of(s * span, span), span), :],
                    outs[r].at[0, d, pl.ds(pl.multiple_of(s * span, span), span), :],
                    sems.at[r],
                ).start()
                return carry

            lax.fori_loop(0, tiles // group, tile, 0)
            base += held
    for r in range(levels):
        pltpu.make_async_copy(obufs[r], outs[r].at[0], sems.at[r]).wait()


def filters(xe, basis, lead, levels):
    rows = xe.shape[0]
    length, width = basis.shape
    samples = (rows // 2 - lead) * LANES
    held = sum(
        2 * ((samples >> r) // LANES + max(1, (length >> r) // LANES) - 1) for r in range(levels)
    )
    vm = lambda: pl.BlockSpec(memory_space=pltpu.VMEM)
    return pl.pallas_call(
        functools.partial(filter_kernel, lead),
        out_shape=[
            jax.ShapeDtypeStruct((1, 2, samples >> r, width), bf16) for r in range(levels)
        ],
        in_specs=[vm(), vm()],
        out_specs=[pl.BlockSpec(memory_space=pl.ANY)] * levels,
        scratch_shapes=[pltpu.VMEM((rows >> r, LANES), f32) for r in range(levels)]
        + [pltpu.VMEM((width // LANES, length, LANES), f32), pltpu.VMEM((LANES, held * LANES), bf16)]
        + [pltpu.VMEM((2, samples >> r, width), bf16) for r in range(levels)]
        + [pltpu.SemaphoreType.DMA((levels,))],
        compiler_params=pltpu.CompilerParams(vmem_limit_bytes=VMEM_LIMIT),
        name="filters",
    )(xe, basis)


def mixing_kernel(bins, white_ref, code_ref, bases_ref, out_ref):
    rows = white_ref.shape[0]
    white = white_ref[...]
    bin_col = jnp.transpose(jnp.broadcast_to(code_ref[...] // 8, (8, rows)).astype(f32))[:, 0:1]
    acc = None
    for b in range(bins):
        mixed = dot(white, bases_ref[b], 1, 0)
        acc = mixed if acc is None else jnp.where(bin_col == float(b), mixed, acc)
    out_ref[...] = acc.astype(bf16)


def local(bins, group_size, templates, owner_device, rate_code, rate_gains, sketch, strain):
    rows, length = templates.shape
    width = sketch.shape[1]
    levels = rate_gains.shape[0]
    lead = 16
    scale = 1.0 / (rows * group_size * math.sqrt(length))
    params = pltpu.CompilerParams(vmem_limit_bytes=VMEM_LIMIT)
    code = (owner_device[:, 0] // group_size * 8 + rate_code)[None, :]
    gains = jnp.concatenate([rate_gains, jnp.zeros((8 - levels, length), f32)], axis=0)
    white, parts = pl.pallas_call(
        functools.partial(partial_kernel, bins),
        out_shape=[
            jax.ShapeDtypeStruct((rows, length), bf16),
            jax.ShapeDtypeStruct((bins, length, width), f32),
        ],
        compiler_params=params,
        name="partials",
    )(templates, code, gains, sketch)
    product = lax.psum_scatter(parts, "bin", scatter_dimension=0, tiled=True)[0]
    product = lax.psum(product, "grp")
    n = LANES
    halo = lax.ppermute(
        strain[:, -lead * n :], "grp", [(i, i + 1) for i in range(group_size - 1)]
    )
    xe = jnp.concatenate([halo, strain], axis=1).reshape(-1, n)
    basis, spectrum = pl.pallas_call(
        functools.partial(basis_kernel, scale),
        out_shape=[
            jax.ShapeDtypeStruct((length, width), bf16),
            jax.ShapeDtypeStruct((1, width), f32),
        ],
        scratch_shapes=[pltpu.VMEM((width, width), f32)] * 2,
        compiler_params=params,
        name="basis",
    )(product)
    bases = lax.all_gather(basis, "bin", axis=0, tiled=False)
    filtered = filters(xe, basis, lead, levels)
    mixing = pl.pallas_call(
        functools.partial(mixing_kernel, bins),
        out_shape=jax.ShapeDtypeStruct((rows, width), bf16),
        compiler_params=params,
        name="mixing",
    )(white, code, bases)
    return (mixing, spectrum, *filtered)


def solution(mesh):
    return jax.shard_map(
        functools.partial(local, mesh.shape["bin"], mesh.shape["grp"]),
        mesh=mesh,
        in_specs=(
            P(("bin", "grp"), None),
            P(("bin", "grp"), None),
            P(("bin", "grp")),
            P(),
            P(),
            P(None, "grp"),
        ),
        out_specs=(P(("bin", "grp"), None), P("bin", None)) + (P("bin", None, "grp", None),) * 5,
        check_vma=False,
    )
```

```python
import functools
import math

import jax
import jax.numpy as jnp
from jax import lax
from jax.experimental import pallas as pl
from jax.experimental.pallas import tpu as pltpu
from jax.sharding import PartitionSpec as P

f32, bf16 = jnp.float32, jnp.bfloat16
highest = lax.Precision.HIGHEST
inv_root_two = 0.7071067811865476
LANES = 128
VMEM_LIMIT = 56 << 20


def dot(a, b, ca, cb, precision=None):
    return lax.dot_general(
        a, b, (((ca,), (cb,)), ((), ())), precision=precision, preferred_element_type=f32
    )


def split(x, parts):
    out = []
    for _ in range(parts):
        piece = x.astype(bf16)
        out.append(piece)
        x = x - piece.astype(f32)
    return out


def product_kernel(
    bins, group_size, planes, lead,
    t_ref, code_ref, gains_ref, sketch_ref, x_ref,
    white_ref, product_ref, xe_ref,
    halves, send1, recv1, send2, recv2, total, send3, recv3, full, edge, sems,
):
    rows, length = t_ref.shape
    half = length // 2
    piece = half // planes
    bin_at, at = lax.axis_index("bin"), lax.axis_index("grp")
    core, place = at % 2, at // 2
    mesh_id = pl.DeviceIdType.MESH
    sibling = (bin_at, place * 2 + 1 - core)
    following = (bin_at, (at + 1) % group_size)
    leading = (bin_at, (at + group_size - 1) % group_size)

    barrier = pltpu.get_barrier_semaphore()

    def greet(device):
        pl.semaphore_signal(barrier, inc=1, device_id=device, device_id_type=mesh_id)

    greet(sibling)
    greet(following)
    greet(leading)
    for k in range(1, bins):
        greet(((bin_at + k) % bins, at))

    @pl.loop(1, planes)
    def _(k):
        greet((bin_at, (place + k) % planes * 2 + core))

    def remote(src, dst, group, index, device):
        return pltpu.make_async_remote_copy(
            src_ref=src, dst_ref=dst, send_sem=sems.at[group, 0, index],
            recv_sem=sems.at[group, 1, index], device_id=device, device_id_type=mesh_id,
        )

    code = code_ref[...]
    rate = jnp.broadcast_to(code % 8, (24, rows))
    which = lax.broadcasted_iota(jnp.int32, (24, rows), 0) % 8
    onehot = jnp.where(rate == which, 1.0, 0.0).astype(bf16)
    gains = jnp.concatenate(split(gains_ref[...], 3), axis=0)
    factor = dot(onehot, gains, 0, 0)
    white = (t_ref[...].astype(f32) * factor).astype(bf16)
    white_ref[...] = white
    sk = split(sketch_ref[...], 2)
    y = dot(white, sk[0], 1, 0) + dot(white, sk[1], 1, 0)
    width = y.shape[1]
    bin_col = jnp.transpose(jnp.broadcast_to(code // 8, (8, rows)).astype(f32))[:, 0:1]
    yh, yl = split(y, 2)
    yh, yl = yh.astype(f32), yl.astype(f32)

    pl.semaphore_wait(barrier, planes + bins + 1)
    xrows = x_ref.shape[0] // 2
    edges = [
        remote(x_ref.at[pl.ds(d * xrows + xrows - lead, lead), :], edge.at[d], 4, d, following)
        for d in range(2)
    ]
    for e in edges:
        e.start()

    first = [remote(send1.at[k], recv1.at[k], 0, k, sibling) for k in range(bins)]
    second = [
        k and remote(send2.at[k], recv2.at[k], 1, k, ((bin_at + k) % bins, at))
        for k in range(bins)
    ]

    def form(k):
        m = bin_col == ((bin_at + k) % bins).astype(f32)
        yb = jnp.concatenate(
            [jnp.where(m, yh, 0.0).astype(bf16), jnp.where(m, yl, 0.0).astype(bf16)], axis=1
        )
        pb = dot(white, yb, 0, 0)
        pb = pb[:, :width] + pb[:, width:]
        halves[k, 0] = pb[:half]
        halves[k, 1] = pb[half:]
        send1[k] = halves[k, 1 - core].astype(bf16)
        first[k].start()

    def join(k):
        first[k].wait_recv()
        both = halves[k, core] + recv1[k].astype(f32)
        if k:
            send2[k] = both.astype(bf16)
            second[k].start()
        return both

    form(1)
    form(2)
    join(1)
    form(3)
    join(2)
    form(0)
    join(3)
    mine = join(0)
    for k in range(1, bins):
        second[k].wait_recv()
        mine = mine + recv2[k].astype(f32)
    total[...] = mine.reshape(planes, piece, width)
    send3[...] = total[...].astype(bf16)

    def third(k):
        target = (place + k) % planes
        return remote(send3.at[target], recv3.at[k], 2, k, (bin_at, target * 2 + core))

    @pl.loop(1, planes)
    def _(k):
        third(k).start()

    @pl.loop(1, planes)
    def _(k):
        third(k).wait_recv()

    acc = total[place]
    for k in range(1, planes):
        acc = acc + recv3[k].astype(f32)
    full[core, place] = acc

    def fourth(k):
        target = (place + k) % planes
        return remote(
            full.at[core, place], full.at[core, place], 3, k, (bin_at, target * 2 + core)
        )

    @pl.loop(1, planes)
    def _(k):
        fourth(k).start()

    @pl.loop(1, planes)
    def _(k):
        fourth(k).wait_recv()

    last = remote(full.at[core], full.at[core], 4, 2, sibling)
    last.start()
    for d in range(2):
        edges[d].wait_recv()
        xe_ref[pl.ds(d * (xrows + lead), lead), :] = jnp.where(at > 0, edge[d], 0.0)
        xe_ref[pl.ds(d * (xrows + lead) + lead, xrows), :] = x_ref[pl.ds(d * xrows, xrows), :]
        edges[d].wait_send()
    for k in range(bins):
        first[k].wait_send()
    for k in range(1, bins):
        second[k].wait_send()

    @pl.loop(1, planes)
    def _(k):
        third(k).wait_send()
        fourth(k).wait_send()

    last.wait()
    product_ref[...] = full[...].reshape(length, width)


def products(bins, group_size, lead, templates, code, gains, sketch, x):
    rows, length = templates.shape
    width = sketch.shape[1]
    planes = group_size // 2
    half, piece = length // 2, length // group_size
    vm = lambda: pl.BlockSpec(memory_space=pltpu.VMEM)
    return pl.pallas_call(
        functools.partial(product_kernel, bins, group_size, planes, lead),
        out_shape=[
            jax.ShapeDtypeStruct((rows, length), bf16),
            jax.ShapeDtypeStruct((length, width), f32),
            jax.ShapeDtypeStruct((x.shape[0] + 2 * lead, LANES), f32),
        ],
        in_specs=[vm() for _ in range(5)],
        out_specs=[vm() for _ in range(3)],
        scratch_shapes=[
            pltpu.VMEM((bins, 2, half, width), f32),
            pltpu.VMEM((bins, half, width), bf16),
            pltpu.VMEM((bins, half, width), bf16),
            pltpu.VMEM((bins, half, width), bf16),
            pltpu.VMEM((bins, half, width), bf16),
            pltpu.VMEM((planes, piece, width), f32),
            pltpu.VMEM((planes, piece, width), bf16),
            pltpu.VMEM((planes, piece, width), bf16),
            pltpu.VMEM((2, planes, piece, width), f32),
            pltpu.VMEM((2, lead, LANES), f32),
            pltpu.SemaphoreType.DMA((5, 2, planes)),
        ],
        compiler_params=pltpu.CompilerParams(
            vmem_limit_bytes=VMEM_LIMIT, collective_id=0, has_side_effects=True
        ),
        name="products",
    )(templates, code, gains, sketch, x)


def eliminate(D, nb, w=8):
    groups = nb // 8
    W2 = 2 * nb
    ri = lax.broadcasted_iota(jnp.int32, (nb, nb), 0)
    ci = lax.broadcasted_iota(jnp.int32, (nb, nb), 1)
    eye = jnp.where(ri == ci, 1.0, 0.0).astype(f32)
    M = jnp.concatenate([D, eye], axis=1)
    Mv = [M[8 * k : 8 * k + 8, :] for k in range(groups)]
    sub = lax.broadcasted_iota(jnp.int32, (8, W2), 0)
    spread = lambda x: jnp.broadcast_to(x, (8, W2))
    for j in range(0, nb, w):
        g = j // 8
        a = [spread(Mv[(j + s) // 8][(j + s) % 8 : (j + s) % 8 + 1, :]) for s in range(w)]
        S = [
            [spread(a[s][:, j + t : j + t + 1]) if t >= s else None for t in range(w)]
            for s in range(w)
        ]
        c = {k: [spread(Mv[k][:, j + s : j + s + 1]) for s in range(w)] for k in range(g, groups)}
        inv = []
        for s in range(w):
            iv = 1.0 / S[s][s]
            inv.append(iv)
            for t in range(s + 1, w):
                f = S[s][t] * iv
                for u in range(t, w):
                    S[t][u] = S[t][u] - f * S[s][u]
                a[t] = a[t] - f * a[s]
        for k in range(g, groups):
            acc = Mv[k]
            for s in range(w):
                m = c[k][s] * inv[s]
                if k * 8 <= j + s:
                    m = jnp.where(sub + 8 * k > j + s, m, 0.0)
                acc = acc - m * a[s]
                for t in range(s + 1, w):
                    c[k][t] = c[k][t] - m * S[s][t]
            Mv[k] = acc
    M = jnp.concatenate(Mv, axis=0)
    diag = jnp.where(ri == ci, M[:, :nb], 0.0)
    d_col = jnp.sum(diag, axis=1, keepdims=True)
    d_row = jnp.sum(diag, axis=0, keepdims=True)
    return M[:, nb:] * lax.rsqrt(d_col), d_row * lax.rsqrt(d_row)


def basis_steps(product, scale, A, X, spec_ref):
    n, nb = product.shape[1], 128
    A[...] = dot(product, product, 0, 0, highest)
    X0, d0 = eliminate(A[:nb, :nb], nb)
    R = dot(X0, A[:nb, nb:], 1, 0, highest)
    X1, d1 = eliminate(A[nb:, nb:] - dot(R, R, 0, 0, highest), nb)
    X[:nb, :nb] = X0
    X[:nb, nb:] = jnp.zeros((nb, n - nb), f32)
    X[nb:, nb:] = X1
    X[nb:, :nb] = -dot(X1, dot(R, X0, 0, 0, highest), 1, 0, highest)
    spec_ref[...] = jnp.concatenate([d0, d1], axis=1) * scale
    return dot(product, X[...], 1, 1, highest).astype(bf16)


def basis_kernel(scale, p_ref, basis_ref, spec_ref, A, X):
    basis_ref[...] = basis_steps(p_ref[...], scale, A, X, spec_ref)


def filter_kernel(lead, xe_ref, basis_ref, *rest):
    outs, (rv0, rv1, rv2, rv3, rv4, bwide, strip), (o0, o1, o2, o3, o4), sems = (
        rest[:5], rest[5:12], rest[12:17], rest[17]
    )
    rvs, obufs = (rv0, rv1, rv2, rv3, rv4), (o0, o1, o2, o3, o4)
    levels = len(outs)
    n = LANES
    ri = lax.broadcasted_iota(jnp.int32, (n, n), 0)
    ci = lax.broadcasted_iota(jnp.int32, (n, n), 1)
    flip = jnp.where(ri + ci == n - 1, 1.0, 0.0).astype(f32)
    first = jnp.where(ri // 2 == ci, 1.0, 0.0).astype(f32)
    second = jnp.where(ri // 2 == ci - n // 2, 1.0, 0.0).astype(f32)
    rv0[...] = dot(xe_ref[...], flip, 1, 0, highest)
    for r in range(1, levels):
        count = rvs[r].shape[0]
        later = rvs[r - 1][pl.ds(1, count, stride=2), :]
        earlier = rvs[r - 1][pl.ds(0, count, stride=2), :]
        rvs[r][...] = (
            dot(later, first, 1, 0, highest) + dot(earlier, second, 1, 0, highest)
        ) * inv_root_two
    for h in range(bwide.shape[0]):
        bwide[h] = basis_ref[:, h * n : (h + 1) * n].astype(f32)

    def every(taps, step):
        halves = [bwide[h, pl.ds(0, taps, stride=step), :] for h in range(bwide.shape[0])]
        return jnp.concatenate(halves, axis=1)

    length, width = basis_ref.shape
    base = 0
    copies = []
    for r in range(levels):
        taps = length >> r
        blocks = max(1, taps // n)
        rows = rvs[r].shape[0] // 2
        head = lead >> r
        tiles = rows - head
        held = tiles + blocks - 1
        if taps >= n:
            weight = every(taps, 1 << r).astype(bf16) if r else basis_ref[...]
        else:
            weight = jnp.concatenate(
                [every(taps, 1 << r), jnp.zeros((n - taps, width), f32)], axis=0
            ).astype(bf16)
        bwide_r = weight
        group = min(8, tiles)
        for d in range(2):
            first_col = base

            def build(p, carry, r=r, d=d, rows=rows, first_col=first_col):
                q = d * rows + rows - 1 - p
                z = jnp.concatenate(
                    [rvs[r][pl.ds(q, 1), :], rvs[r][pl.ds(q - 1, 1), :]], axis=1
                ).astype(bf16).astype(f32)
                z = jnp.broadcast_to(z, (n, 2 * n))
                t = pltpu.roll(z, n + 1, 1, stride=1, stride_axis=0)[:, :n]
                strip[:, pl.ds(pl.multiple_of((first_col + p) * n, n), n)] = t.astype(bf16)
                return carry

            lax.fori_loop(0, held, build, 0)

            def tile(s, carry, r=r, d=d, rows=rows, first_col=first_col, group=group,
                     blocks=blocks, weight=bwide_r, tiles=tiles):
                parts = []
                for i in range(group):
                    p = first_col + tiles - 1 - (s * group + i)
                    parts.append(strip[:, pl.ds(pl.multiple_of(p * n, n), blocks * n)])
                lhs = jnp.concatenate(parts, axis=0)
                span = group * n
                obufs[r][d, pl.ds(pl.multiple_of(s * span, span), span), :] = dot(
                    lhs, weight, 1, 0
                ).astype(bf16)
                pltpu.make_async_copy(
                    obufs[r].at[d, pl.ds(pl.multiple_of(s * span, span), span), :],
                    outs[r].at[0, d, pl.ds(pl.multiple_of(s * span, span), span), :],
                    sems.at[r],
                ).start()
                return carry

            lax.fori_loop(0, tiles // group, tile, 0)
            base += held
    for r in range(levels):
        pltpu.make_async_copy(obufs[r], outs[r].at[0], sems.at[r]).wait()


def filters(xe, basis, lead, levels):
    rows = xe.shape[0]
    length, width = basis.shape
    samples = (rows // 2 - lead) * LANES
    held = sum(
        2 * ((samples >> r) // LANES + max(1, (length >> r) // LANES) - 1) for r in range(levels)
    )
    vm = lambda: pl.BlockSpec(memory_space=pltpu.VMEM)
    return pl.pallas_call(
        functools.partial(filter_kernel, lead),
        out_shape=[
            jax.ShapeDtypeStruct((1, 2, samples >> r, width), bf16) for r in range(levels)
        ],
        in_specs=[vm(), vm()],
        out_specs=[pl.BlockSpec(memory_space=pl.ANY)] * levels,
        scratch_shapes=[pltpu.VMEM((rows >> r, LANES), f32) for r in range(levels)]
        + [pltpu.VMEM((width // LANES, length, LANES), f32), pltpu.VMEM((LANES, held * LANES), bf16)]
        + [pltpu.VMEM((2, samples >> r, width), bf16) for r in range(levels)]
        + [pltpu.SemaphoreType.DMA((levels,))],
        compiler_params=pltpu.CompilerParams(vmem_limit_bytes=VMEM_LIMIT),
        name="filters",
    )(xe, basis)


def mixing_kernel(bins, white_ref, code_ref, bases_ref, out_ref):
    rows = white_ref.shape[0]
    white = white_ref[...]
    bin_col = jnp.transpose(jnp.broadcast_to(code_ref[...] // 8, (8, rows)).astype(f32))[:, 0:1]
    acc = None
    for b in range(bins):
        mixed = dot(white, bases_ref[b], 1, 0)
        acc = mixed if acc is None else jnp.where(bin_col == float(b), mixed, acc)
    out_ref[...] = acc.astype(bf16)


def local(bins, group_size, templates, owner_device, rate_code, rate_gains, sketch, strain):
    rows, length = templates.shape
    width = sketch.shape[1]
    levels = rate_gains.shape[0]
    lead = 16
    scale = 1.0 / (rows * group_size * math.sqrt(length))
    params = pltpu.CompilerParams(vmem_limit_bytes=VMEM_LIMIT)
    code = (owner_device[:, 0] // group_size * 8 + rate_code)[None, :]
    gains = jnp.concatenate([rate_gains, jnp.zeros((8 - levels, length), f32)], axis=0)
    x = strain.reshape(-1, LANES)
    white, product, xe = products(bins, group_size, lead, templates, code, gains, sketch, x)
    basis, spectrum = pl.pallas_call(
        functools.partial(basis_kernel, scale),
        out_shape=[
            jax.ShapeDtypeStruct((length, width), bf16),
            jax.ShapeDtypeStruct((1, width), f32),
        ],
        scratch_shapes=[pltpu.VMEM((width, width), f32)] * 2,
        compiler_params=params,
        name="basis",
    )(product)
    bases = lax.all_gather(basis, "bin", axis=0, tiled=False)
    filtered = filters(xe, basis, lead, levels)
    mixing = pl.pallas_call(
        functools.partial(mixing_kernel, bins),
        out_shape=jax.ShapeDtypeStruct((rows, width), bf16),
        compiler_params=params,
        name="mixing",
    )(white, code, bases)
    return (mixing, spectrum, *filtered)


def solution(mesh):
    return jax.shard_map(
        functools.partial(local, mesh.shape["bin"], mesh.shape["grp"]),
        mesh=mesh,
        in_specs=(
            P(("bin", "grp"), None),
            P(("bin", "grp"), None),
            P(("bin", "grp")),
            P(),
            P(),
            P(None, "grp"),
        ),
        out_specs=(P(("bin", "grp"), None), P("bin", None)) + (P("bin", None, "grp", None),) * 5,
        check_vma=False,
    )
```

```python
import functools
import math

import jax
import jax.numpy as jnp
from jax import lax
from jax.experimental import pallas as pl
from jax.experimental.pallas import tpu as pltpu
from jax.sharding import PartitionSpec as P

f32, bf16 = jnp.float32, jnp.bfloat16
highest = lax.Precision.HIGHEST
inv_root_two = 0.7071067811865476
LANES = 128
VMEM_LIMIT = 56 << 20


def dot(a, b, ca, cb, precision=None):
    return lax.dot_general(
        a, b, (((ca,), (cb,)), ((), ())), precision=precision, preferred_element_type=f32
    )


def split(x, parts):
    out = []
    for _ in range(parts):
        piece = x.astype(bf16)
        out.append(piece)
        x = x - piece.astype(f32)
    return out


def product_kernel(
    bins, group_size, planes, lead, plan, levels,
    t_ref, code_ref, gains_ref, sketch_ref, x_ref,
    white_ref, product_ref, strip_ref,
    halves, send1, recv1, send2, recv2, total, send3, recv3, full, edge, xe, strip, *rest,
):
    rvs, sems, strip_sem = rest[:levels], rest[levels], rest[levels + 1]
    rows, length = t_ref.shape
    half = length // 2
    piece = half // planes
    bin_at, at = lax.axis_index("bin"), lax.axis_index("grp")
    core, place = at % 2, at // 2
    mesh_id = pl.DeviceIdType.MESH
    sibling = (bin_at, place * 2 + 1 - core)
    following = (bin_at, (at + 1) % group_size)
    leading = (bin_at, (at + group_size - 1) % group_size)

    barrier = pltpu.get_barrier_semaphore()

    def greet(device):
        pl.semaphore_signal(barrier, inc=1, device_id=device, device_id_type=mesh_id)

    greet(sibling)
    greet(following)
    greet(leading)
    for k in range(1, bins):
        greet(((bin_at + k) % bins, at))

    @pl.loop(1, planes)
    def _(k):
        greet((bin_at, (place + k) % planes * 2 + core))

    def remote(src, dst, group, index, device):
        return pltpu.make_async_remote_copy(
            src_ref=src, dst_ref=dst, send_sem=sems.at[group, 0, index],
            recv_sem=sems.at[group, 1, index], device_id=device, device_id_type=mesh_id,
        )

    code = code_ref[...]
    rate = jnp.broadcast_to(code % 8, (24, rows))
    which = lax.broadcasted_iota(jnp.int32, (24, rows), 0) % 8
    onehot = jnp.where(rate == which, 1.0, 0.0).astype(bf16)
    gains = jnp.concatenate(
        [gains_ref[...], jnp.zeros((8 - levels, length), f32)], axis=0
    )
    gains = jnp.concatenate(split(gains, 3), axis=0)
    factor = dot(onehot, gains, 0, 0)
    white = (t_ref[...].astype(f32) * factor).astype(bf16)
    white_ref[...] = white
    sk = split(sketch_ref[...], 2)
    y = dot(white, sk[0], 1, 0) + dot(white, sk[1], 1, 0)
    width = y.shape[1]
    bin_col = jnp.transpose(jnp.broadcast_to(code // 8, (8, rows)).astype(f32))[:, 0:1]
    yh, yl = split(y, 2)
    yh, yl = yh.astype(f32), yl.astype(f32)

    pl.semaphore_wait(barrier, planes + bins + 1)
    xrows = x_ref.shape[1] // LANES
    for d in range(2):
        for i in range(xrows):
            xe[pl.ds(d * (xrows + lead) + lead + i, 1), :] = x_ref[
                d : d + 1, i * LANES : (i + 1) * LANES
            ]
    edges = [
        remote(
            xe.at[pl.ds(d * (xrows + lead) + xrows, lead), :], edge.at[d], 4, d, following
        )
        for d in range(2)
    ]
    for e in edges:
        e.start()

    first = [remote(send1.at[k], recv1.at[k], 0, k, sibling) for k in range(bins)]
    second = [
        k and remote(send2.at[k], recv2.at[k], 1, k, ((bin_at + k) % bins, at))
        for k in range(bins)
    ]

    def form(k):
        m = bin_col == float(k)
        yb = jnp.concatenate(
            [jnp.where(m, yh, 0.0).astype(bf16), jnp.where(m, yl, 0.0).astype(bf16)], axis=1
        )
        pb = dot(white, yb, 0, 0)
        pb = pb[:, :width] + pb[:, width:]
        halves[k, 0] = pb[:half]
        halves[k, 1] = pb[half:]
        send1[k] = halves[k, 1 - core].astype(bf16)
        first[k].start()

    def join(k):
        first[k].wait_recv()
        both = halves[k, core] + recv1[k].astype(f32)
        if k:
            send2[k] = both.astype(bf16)
            second[k].start()
        return both

    form(1)
    form(2)
    join(1)
    form(3)
    join(2)
    form(0)
    join(3)
    mine = join(0)
    for d in range(2):
        edges[d].wait_recv()
        xe[pl.ds(d * (xrows + lead), lead), :] = jnp.where(at > 0, edge[d], 0.0)
    decimate(rvs, xe[...])
    for entry in plan[:2]:
        build_strip(entry, rvs[entry[0]], strip)
    for k in range(1, bins):
        second[k].wait_recv()
        mine = mine + recv2[k].astype(f32)
    total[...] = mine.reshape(planes, piece, width)
    send3[...] = total[...].astype(bf16)

    def third(k):
        target = (place + k) % planes
        return remote(send3.at[target], recv3.at[k], 2, k, (bin_at, target * 2 + core))

    @pl.loop(1, planes)
    def _(k):
        third(k).start()

    for entry in plan[2:]:
        build_strip(entry, rvs[entry[0]], strip)
    store = pltpu.make_async_copy(strip, strip_ref, strip_sem)
    store.start()

    @pl.loop(1, planes)
    def _(k):
        third(k).wait_recv()

    acc = total[place]
    for k in range(1, planes):
        acc = acc + recv3[k].astype(f32)
    full[core, place] = acc

    def fourth(k):
        target = (place + k) % planes
        return remote(
            full.at[core, place], full.at[core, place], 3, k, (bin_at, target * 2 + core)
        )

    @pl.loop(1, planes)
    def _(k):
        fourth(k).start()

    @pl.loop(1, planes)
    def _(k):
        fourth(k).wait_recv()

    last = remote(full.at[core], full.at[core], 4, 2, sibling)
    last.start()
    for d in range(2):
        edges[d].wait_send()
    for k in range(bins):
        first[k].wait_send()
    for k in range(1, bins):
        second[k].wait_send()

    @pl.loop(1, planes)
    def _(k):
        third(k).wait_send()
        fourth(k).wait_send()

    last.wait()
    store.wait()
    product_ref[...] = full[...].reshape(length, width)


def products(bins, group_size, lead, plan, held, templates, code, gains, sketch, strain):
    rows, length = templates.shape
    width = sketch.shape[1]
    levels = gains.shape[0]
    planes = group_size // 2
    half, piece = length // 2, length // group_size
    xrows = strain.shape[1] // LANES + lead
    vm = lambda: pl.BlockSpec(memory_space=pltpu.VMEM)
    return pl.pallas_call(
        functools.partial(product_kernel, bins, group_size, planes, lead, plan, levels),
        out_shape=[
            jax.ShapeDtypeStruct((rows, length), bf16),
            jax.ShapeDtypeStruct((length, width), f32),
            jax.ShapeDtypeStruct((LANES, held * LANES), bf16),
        ],
        in_specs=[vm() for _ in range(5)],
        out_specs=[vm(), vm(), pl.BlockSpec(memory_space=pl.ANY)],
        scratch_shapes=[
            pltpu.VMEM((bins, 2, half, width), f32),
            pltpu.VMEM((bins, half, width), bf16),
            pltpu.VMEM((bins, half, width), bf16),
            pltpu.VMEM((bins, half, width), bf16),
            pltpu.VMEM((bins, half, width), bf16),
            pltpu.VMEM((planes, piece, width), f32),
            pltpu.VMEM((planes, piece, width), bf16),
            pltpu.VMEM((planes, piece, width), bf16),
            pltpu.VMEM((2, planes, piece, width), f32),
            pltpu.VMEM((2, lead, LANES), f32),
            pltpu.VMEM((2 * xrows, LANES), f32),
            pltpu.VMEM((LANES, held * LANES), bf16),
        ]
        + [pltpu.VMEM((2 * xrows >> r, LANES), f32) for r in range(levels)]
        + [pltpu.SemaphoreType.DMA((5, 2, planes)), pltpu.SemaphoreType.DMA],
        compiler_params=pltpu.CompilerParams(
            vmem_limit_bytes=VMEM_LIMIT, collective_id=0, has_side_effects=True
        ),
        name="products",
    )(templates, code, gains, sketch, strain)


def eliminate(D, nb, w=8):
    groups = nb // 8
    W2 = 2 * nb
    ri = lax.broadcasted_iota(jnp.int32, (nb, nb), 0)
    ci = lax.broadcasted_iota(jnp.int32, (nb, nb), 1)
    eye = jnp.where(ri == ci, 1.0, 0.0).astype(f32)
    M = jnp.concatenate([D, eye], axis=1)
    Mv = [M[8 * k : 8 * k + 8, :] for k in range(groups)]
    sub = lax.broadcasted_iota(jnp.int32, (8, W2), 0)
    spread = lambda x: jnp.broadcast_to(x, (8, W2))
    for j in range(0, nb, w):
        g = j // 8
        a = [spread(Mv[(j + s) // 8][(j + s) % 8 : (j + s) % 8 + 1, :]) for s in range(w)]
        S = [
            [spread(a[s][:, j + t : j + t + 1]) if t >= s else None for t in range(w)]
            for s in range(w)
        ]
        c = {k: [spread(Mv[k][:, j + s : j + s + 1]) for s in range(w)] for k in range(g, groups)}
        inv = []
        for s in range(w):
            iv = 1.0 / S[s][s]
            inv.append(iv)
            for t in range(s + 1, w):
                f = S[s][t] * iv
                for u in range(t, w):
                    S[t][u] = S[t][u] - f * S[s][u]
                a[t] = a[t] - f * a[s]
        for k in range(g, groups):
            acc = Mv[k]
            for s in range(w):
                m = c[k][s] * inv[s]
                if k * 8 <= j + s:
                    m = jnp.where(sub + 8 * k > j + s, m, 0.0)
                acc = acc - m * a[s]
                for t in range(s + 1, w):
                    c[k][t] = c[k][t] - m * S[s][t]
            Mv[k] = acc
    M = jnp.concatenate(Mv, axis=0)
    diag = jnp.where(ri == ci, M[:, :nb], 0.0)
    d_col = jnp.sum(diag, axis=1, keepdims=True)
    d_row = jnp.sum(diag, axis=0, keepdims=True)
    return M[:, nb:] * lax.rsqrt(d_col), d_row * lax.rsqrt(d_row)


def basis_steps(product, scale, A, X, spec_ref):
    n, nb = product.shape[1], 128
    A[...] = dot(product, product, 0, 0, highest)
    X0, d0 = eliminate(A[:nb, :nb], nb)
    R = dot(X0, A[:nb, nb:], 1, 0, highest)
    X1, d1 = eliminate(A[nb:, nb:] - dot(R, R, 0, 0, highest), nb)
    X[:nb, :nb] = X0
    X[:nb, nb:] = jnp.zeros((nb, n - nb), f32)
    X[nb:, nb:] = X1
    X[nb:, :nb] = -dot(X1, dot(R, X0, 0, 0, highest), 1, 0, highest)
    spec_ref[...] = jnp.concatenate([d0, d1], axis=1) * scale
    return dot(product, X[...], 1, 1, highest).astype(bf16)


def basis_kernel(scale, p_ref, basis_ref, spec_ref, A, X):
    basis_ref[...] = basis_steps(p_ref[...], scale, A, X, spec_ref)


def strip_plan(tiles, length, levels, lead):
    plan, base = [], 0
    for r in range(levels):
        blocks = max(1, (length >> r) // LANES)
        rows = (tiles + lead) >> r
        held = (tiles >> r) + blocks - 1
        chunk = next(m for m in (17, 16, 8, 4, 2, 1) if held % m == 0 or (m == 17 and held > 17 and held % 17 >= 15))
        for d in range(2):
            plan.append((r, d, tiles >> r, blocks, rows, chunk, -(-held // chunk), base))
            base += -(-held // chunk) * chunk
    return plan, base


def decimate(rvs, x):
    n = LANES
    ri = lax.broadcasted_iota(jnp.int32, (n, n), 0)
    ci = lax.broadcasted_iota(jnp.int32, (n, n), 1)
    flip = jnp.where(ri + ci == n - 1, 1.0, 0.0).astype(f32)
    first = jnp.where(ri // 2 == ci, 1.0, 0.0).astype(f32)
    second = jnp.where(ri // 2 == ci - n // 2, 1.0, 0.0).astype(f32)
    rvs[0][...] = dot(x, flip, 1, 0, highest)
    for r in range(1, len(rvs)):
        count = rvs[r].shape[0]
        later = rvs[r - 1][pl.ds(1, count, stride=2), :]
        earlier = rvs[r - 1][pl.ds(0, count, stride=2), :]
        rvs[r][...] = (
            dot(later, first, 1, 0, highest) + dot(earlier, second, 1, 0, highest)
        ) * inv_root_two


def build_strip(entry, rv, strip):
    r, d, tiles, blocks, rows, chunk, count, base = entry
    n = LANES
    wide = chunk + 1
    span = (wide + 1) * n

    def step(i, carry):
        q = d * rows + rows - 1 - i * chunk
        z = jnp.concatenate(
            [rv[pl.ds(jnp.maximum(q - j, 0), 1), :] for j in range(wide + 1)], axis=1
        ).astype(bf16).astype(f32)
        z = jnp.broadcast_to(z, (16, span))
        z = pltpu.roll(z, span - 15, 1, stride=1, stride_axis=0)[:, : wide * n]
        at = pl.ds(pl.multiple_of((base + i * chunk) * n, n), chunk * n)
        for g in range(n // 16):
            k = n - 16 - 16 * g
            t = pltpu.roll(z, wide * n - k, 1) if k else z
            strip[16 * g : 16 * g + 16, at] = t[:, : chunk * n].astype(bf16)
        return carry

    lax.fori_loop(0, count, step, 0)


def filter_kernel(plan, levels, strip_ref, basis_ref, *rest):
    outs, bwide, strip, obufs, in_sems, sems = (
        rest[:levels], rest[levels], rest[levels + 1],
        rest[levels + 2 : 2 * levels + 2], rest[-2], rest[-1],
    )
    n = LANES
    length, width = basis_ref.shape
    loads = []
    for i, (r, d, tiles, blocks, rows, chunk, count, base) in enumerate(plan):
        at = pl.ds(base * n, count * chunk * n)
        loads.append(pltpu.make_async_copy(strip_ref.at[:, at], strip.at[:, at], in_sems.at[i]))
        loads[-1].start()
    for h in range(bwide.shape[0]):
        bwide[h] = basis_ref[:, h * n : (h + 1) * n].astype(f32)

    def every(taps, step):
        halves = [bwide[h, pl.ds(0, taps, stride=step), :] for h in range(bwide.shape[0])]
        return jnp.concatenate(halves, axis=1)

    for i, (r, d, tiles, blocks, rows, chunk, count, base) in enumerate(plan):
        taps = length >> r
        if r == 0:
            weight = basis_ref[...]
        elif taps >= n:
            weight = every(taps, 1 << r).astype(bf16)
        else:
            weight = jnp.concatenate(
                [every(taps, 1 << r), jnp.zeros((n - taps, width), f32)], axis=0
            ).astype(bf16)
        group = min(32, tiles)
        span = group * n
        loads[i].wait()

        def tile(s, carry, r=r, d=d, tiles=tiles, blocks=blocks, base=base, group=group, span=span,
                 weight=weight):
            parts = []
            for t in range(group):
                p = base + tiles - 1 - (s * group + t)
                parts.append(strip[:, pl.ds(pl.multiple_of(p * n, n), blocks * n)])
            at = pl.ds(pl.multiple_of(s * span, span), span)
            obufs[r][d, at, :] = dot(jnp.concatenate(parts, axis=0), weight, 1, 0).astype(bf16)
            pltpu.make_async_copy(
                obufs[r].at[d, at, :], outs[r].at[0, d, at, :], sems.at[r]
            ).start()
            return carry

        lax.fori_loop(0, tiles // group, tile, 0)
    for r in range(levels):
        pltpu.make_async_copy(obufs[r], outs[r].at[0], sems.at[r]).wait()


def filters(plan, held, strip, basis, levels):
    length, width = basis.shape
    samples = plan[0][2] * LANES
    return pl.pallas_call(
        functools.partial(filter_kernel, plan, levels),
        out_shape=[
            jax.ShapeDtypeStruct((1, 2, samples >> r, width), bf16) for r in range(levels)
        ],
        in_specs=[pl.BlockSpec(memory_space=pl.ANY), pl.BlockSpec(memory_space=pltpu.VMEM)],
        out_specs=[pl.BlockSpec(memory_space=pl.ANY)] * levels,
        scratch_shapes=[
            pltpu.VMEM((width // LANES, length, LANES), f32),
            pltpu.VMEM((LANES, held * LANES), bf16),
        ]
        + [pltpu.VMEM((2, samples >> r, width), bf16) for r in range(levels)]
        + [pltpu.SemaphoreType.DMA((len(plan),)), pltpu.SemaphoreType.DMA((levels,))],
        compiler_params=pltpu.CompilerParams(vmem_limit_bytes=VMEM_LIMIT),
        cost_estimate=pl.CostEstimate(
            flops=2 * 2 * samples * length * width, bytes_accessed=26 << 20, transcendentals=0
        ),
        name="filters",
    )(strip, basis)


def mixing_kernel(bins, white_ref, code_ref, *rest):
    bases, out_ref = rest[:bins], rest[bins]
    rows = white_ref.shape[0]
    white = white_ref[...]
    bin_col = jnp.transpose(jnp.broadcast_to(code_ref[...] // 8, (8, rows)).astype(f32))[:, 0:1]
    acc = dot(white, bases[0][...], 1, 0)
    for k in range(1, bins):
        acc = jnp.where(bin_col == float(k), dot(white, bases[k][...], 1, 0), acc)
    out_ref[...] = acc.astype(bf16)


def local(bins, group_size, templates, owner_device, rate_code, rate_gains, sketch, strain):
    rows, length = templates.shape
    width = sketch.shape[1]
    levels = rate_gains.shape[0]
    lead = 16
    scale = 1.0 / (rows * group_size * math.sqrt(length))
    params = pltpu.CompilerParams(vmem_limit_bytes=24 << 20)
    relative = (owner_device[:, 0] // group_size + bins - lax.axis_index("bin")) % bins
    code = (relative * 8 + rate_code)[None, :]
    plan, held = strip_plan(strain.shape[1] // LANES, length, levels, lead)
    white, product, strip = products(
        bins, group_size, lead, plan, held, templates, code, rate_gains, sketch, strain
    )
    basis, spectrum = pl.pallas_call(
        functools.partial(basis_kernel, scale),
        out_shape=[
            jax.ShapeDtypeStruct((length, width), bf16),
            jax.ShapeDtypeStruct((1, width), f32),
        ],
        scratch_shapes=[pltpu.VMEM((width, width), f32)] * 2,
        compiler_params=params,
        name="basis",
    )(product)
    others = [
        lax.ppermute(basis, "bin", [(i, (i - k) % bins) for i in range(bins)])
        for k in range(1, bins)
    ]
    filtered = filters(plan, held, strip, basis, levels)
    mixing = pl.pallas_call(
        functools.partial(mixing_kernel, bins),
        out_shape=jax.ShapeDtypeStruct((rows, width), bf16),
        compiler_params=params,
        name="mixing",
    )(white, code, basis, *others)
    return (mixing, spectrum, *filtered)


def solution(mesh):
    return jax.shard_map(
        functools.partial(local, mesh.shape["bin"], mesh.shape["grp"]),
        mesh=mesh,
        in_specs=(
            P(("bin", "grp"), None),
            P(("bin", "grp"), None),
            P(("bin", "grp")),
            P(),
            P(),
            P(None, "grp"),
        ),
        out_specs=(P(("bin", "grp"), None), P("bin", None)) + (P("bin", None, "grp", None),) * 5,
        check_vma=False,
    )
```

```python
import functools
import math

import jax
import jax.numpy as jnp
from jax import lax
from jax.experimental import pallas as pl
from jax.experimental.pallas import tpu as pltpu
from jax.sharding import PartitionSpec as P

f32, bf16 = jnp.float32, jnp.bfloat16
highest = lax.Precision.HIGHEST
inv_root_two = 0.7071067811865476
LANES = 128


def dot(a, b, ca, cb, precision=None):
    return lax.dot_general(
        a, b, (((ca,), (cb,)), ((), ())), precision=precision, preferred_element_type=f32
    )


def split(x, parts):
    out = []
    for _ in range(parts):
        piece = x.astype(bf16)
        out.append(piece)
        x = x - piece.astype(f32)
    return out


def product_kernel(
    bins, group_size, planes, lead, plan, levels,
    t_hbm, owner_hbm, rate_hbm, gains_hbm, sketch_hbm, x_hbm,
    white_ref, product_ref, strip, bin_ref,
    t_ref, owner_ref, rate_ref, gains_ref, sketch_ref, x_ref,
    halves, send1, recv1, send2, recv2, sendv, recvv, total, send3, recv3, sendy, recvy,
    full, edge, xe, *rest,
):
    rvs, in_sems, sems = rest[:levels], rest[levels], rest[levels + 1]
    rows, length = t_ref.shape
    half = length // 2
    part = half // planes // 2
    bin_at, at = lax.axis_index("bin"), lax.axis_index("grp")
    core, place = at % 2, at // 2
    mesh_id = pl.DeviceIdType.MESH
    sibling = (bin_at, place * 2 + 1 - core)
    following = (bin_at, (at + 1) % group_size)
    leading = (bin_at, (at + group_size - 1) % group_size)

    loads = [
        pltpu.make_async_copy(src, dst, in_sems.at[i])
        for i, (src, dst) in enumerate(
            [
                (x_hbm, x_ref), (gains_hbm, gains_ref), (t_hbm, t_ref), (sketch_hbm, sketch_ref),
                (owner_hbm, owner_ref), (rate_hbm, rate_ref),
            ]
        )
    ]
    for load in loads:
        load.start()
    barrier = pltpu.get_barrier_semaphore()

    def greet(device):
        pl.semaphore_signal(barrier, inc=1, device_id=device, device_id_type=mesh_id)

    greet(sibling)
    greet(following)
    greet(leading)
    for k in range(1, bins):
        greet(((bin_at + k) % bins, at))

    @pl.loop(1, planes)
    def _(k):
        greet((bin_at, (place + k) % planes * 2 + core))

    def remote(src, dst, group, index, device):
        return pltpu.make_async_remote_copy(
            src_ref=src, dst_ref=dst, send_sem=sems.at[group, 0, index],
            recv_sem=sems.at[group, 1, index], device_id=device, device_id_type=mesh_id,
        )

    loads[0].wait()
    xrows = x_ref.shape[1] // LANES
    for d in range(2):
        for i in range(xrows):
            xe[pl.ds(d * (xrows + lead) + lead + i, 1), :] = x_ref[
                d : d + 1, i * LANES : (i + 1) * LANES
            ]
    loads[1].wait()
    gains = jnp.concatenate(
        [gains_ref[...], jnp.zeros((8 - levels, length), f32)], axis=0
    )
    gains = jnp.concatenate(split(gains, 3), axis=0)
    loads[4].wait()
    loads[5].wait()
    relative = (owner_ref[...] // group_size + bins - bin_at) % bins
    bin_ref[...] = relative
    bin_col = jnp.transpose(jnp.broadcast_to(relative, (8, rows)).astype(f32))[:, 0:1]
    rate = jnp.broadcast_to(rate_ref[...], (24, rows))
    which = lax.broadcasted_iota(jnp.int32, (24, rows), 0) % 8
    onehot = jnp.where(rate == which, 1.0, 0.0).astype(bf16)
    factor = dot(onehot, gains, 0, 0)
    loads[2].wait()
    white = (t_ref[...].astype(f32) * factor).astype(bf16)
    white_ref[...] = white
    loads[3].wait()
    sk = split(sketch_ref[...], 2)
    y = dot(white, sk[0], 1, 0) + dot(white, sk[1], 1, 0)
    width = y.shape[1]
    yh, yl = split(y, 2)
    yh, yl = yh.astype(f32), yl.astype(f32)

    pl.semaphore_wait(barrier, planes + bins + 1)
    edges = [
        remote(
            xe.at[pl.ds(d * (xrows + lead) + xrows, lead), :], edge.at[d], 4, bins + d, following
        )
        for d in range(2)
    ]
    for e in edges:
        e.start()

    first = [remote(send1.at[k], recv1.at[k], 0, k, sibling) for k in range(bins)]
    second = [
        k and remote(send2.at[k], recv2.at[k], 1, k, ((bin_at + k) % bins, at))
        for k in range(bins)
    ]
    across = [
        k and remote(sendy.at[k], recvy.at[k], 4, k, ((bin_at + k) % bins, at))
        for k in range(bins)
    ]

    def spread(k):
        target = (place + k) % planes
        return remote(sendv.at[target], recvv.at[k], 2, k, (bin_at, target * 2 + core))

    def third(k):
        target = (place + k) % planes
        return remote(send3.at[target], recv3.at[k], 3, k, (bin_at, target * 2 + core))

    def fourth(k):
        target = (place + k) % planes
        mine = full.at[core, place]
        return remote(mine, mine, 5, k, (bin_at, target * 2 + core))

    def hand(k):
        mine = full.at[core, (place + planes - k) % planes]
        return remote(mine, mine, 6, k, sibling)

    def form(k):
        m = bin_col == float(k)
        yb = jnp.concatenate(
            [jnp.where(m, yh, 0.0).astype(bf16), jnp.where(m, yl, 0.0).astype(bf16)], axis=1
        )
        pb = dot(white, yb, 0, 0)
        pb = pb[:, :width] + pb[:, width:]
        halves[k, 0] = pb[:half]
        halves[k, 1] = pb[half:]
        send1[k] = halves[k, 1 - core].astype(bf16)
        first[k].start()

    def join(k):
        first[k].wait_recv()
        both = (halves[k, core] + recv1[k].astype(f32)).reshape(planes, 2, part, width)
        if k:
            send2[k] = both[:, 0].astype(bf16)
            second[k].start()
        else:
            total[...] = both[:, 0]
        sendv[:, k] = both[:, 1].astype(bf16)

    form(2)
    form(1)
    join(2)
    form(3)
    join(1)
    form(0)
    join(3)
    join(0)

    @pl.loop(1, planes)
    def _(k):
        spread(k).start()

    for d in range(2):
        edges[d].wait_recv()
        xe[pl.ds(d * (xrows + lead), lead), :] = jnp.where(at > 0, edge[d], 0.0)
    decimate(rvs, xe[...])
    for entry in plan[:1]:
        build_strip(entry, rvs[entry[0]], strip)

    for k in range(1, bins):
        second[k].wait_recv()
        total[...] = total[...] + recv2[k].astype(f32)
    send3[...] = total[...].astype(bf16)

    @pl.loop(1, planes)
    def _(k):
        third(k).start()

    @pl.loop(1, planes)
    def _(k):
        spread(k).wait_recv()

    acc = sendv[place].astype(f32)
    for k in range(1, planes):
        acc = acc + recvv[k].astype(f32)
    for k in range(1, bins):
        sendy[k] = acc[k].astype(bf16)
        across[k].start()

    for entry in plan[1:2]:
        build_strip(entry, rvs[entry[0]], strip)

    @pl.loop(1, planes)
    def _(k):
        third(k).wait_recv()

    one = total[place]
    for k in range(1, planes):
        one = one + recv3[k].astype(f32)
    two = acc[0]
    for k in range(1, bins):
        across[k].wait_recv()
        two = two + recvy[k].astype(f32)
    full[core, place] = jnp.concatenate([one, two], axis=0)
    hand(0).start()

    @pl.loop(1, planes)
    def _(k):
        fourth(k).start()

    for entry in plan[2:]:
        build_strip(entry, rvs[entry[0]], strip)

    @pl.loop(1, planes)
    def _(k):
        fourth(k).wait_recv()
        hand(k).start()

    for d in range(2):
        edges[d].wait_send()
    for k in range(bins):
        first[k].wait_send()
    for k in range(1, bins):
        second[k].wait_send()
        across[k].wait_send()

    @pl.loop(1, planes)
    def _(k):
        spread(k).wait_send()
        third(k).wait_send()
        fourth(k).wait_send()

    @pl.loop(0, planes)
    def _(k):
        hand(k).wait()

    product_ref[...] = full[...].reshape(length, width)


def products(bins, group_size, lead, plan, held, templates, owner, rate, gains, sketch, strain):
    rows, length = templates.shape
    width = sketch.shape[1]
    levels = gains.shape[0]
    planes = group_size // 2
    half, part = length // 2, length // group_size // 2
    hbm = lambda: pl.BlockSpec(memory_space=pltpu.HBM)
    xrows = strain.shape[1] // LANES + lead
    vm = lambda: pl.BlockSpec(memory_space=pltpu.VMEM)
    far = lambda a: pltpu.with_memory_space_constraint(a, pltpu.HBM)
    return pl.pallas_call(
        functools.partial(product_kernel, bins, group_size, planes, lead, plan, levels),
        out_shape=[
            jax.ShapeDtypeStruct((rows, length), bf16),
            jax.ShapeDtypeStruct((length, width), f32),
            jax.ShapeDtypeStruct((LANES, held * LANES), bf16),
            jax.ShapeDtypeStruct((1, rows), jnp.int32),
        ],
        in_specs=[hbm() for _ in range(6)],
        out_specs=[vm() for _ in range(4)],
        scratch_shapes=[
            pltpu.VMEM(templates.shape, bf16),
            pltpu.VMEM(owner.shape, jnp.int32),
            pltpu.VMEM(rate.shape, jnp.int32),
            pltpu.VMEM(gains.shape, f32),
            pltpu.VMEM(sketch.shape, f32),
            pltpu.VMEM(strain.shape, f32),
            pltpu.VMEM((bins, 2, half, width), f32),
            pltpu.VMEM((bins, half, width), bf16),
            pltpu.VMEM((bins, half, width), bf16),
            pltpu.VMEM((bins, planes, part, width), bf16),
            pltpu.VMEM((bins, planes, part, width), bf16),
            pltpu.VMEM((planes, bins, part, width), bf16),
            pltpu.VMEM((planes, bins, part, width), bf16),
            pltpu.VMEM((planes, part, width), f32),
            pltpu.VMEM((planes, part, width), bf16),
            pltpu.VMEM((planes, part, width), bf16),
            pltpu.VMEM((bins, part, width), bf16),
            pltpu.VMEM((bins, part, width), bf16),
            pltpu.VMEM((2, planes, 2 * part, width), f32),
            pltpu.VMEM((2, lead, LANES), f32),
            pltpu.VMEM((2 * xrows, LANES), f32),
        ]
        + [pltpu.VMEM((2 * xrows >> r, LANES), f32) for r in range(levels)]
        + [pltpu.SemaphoreType.DMA((6,)), pltpu.SemaphoreType.DMA((7, 2, planes))],
        compiler_params=pltpu.CompilerParams(
            vmem_limit_bytes=30 << 20, collective_id=0, has_side_effects=True
        ),
        name="products",
    )(far(templates), far(owner), far(rate), far(gains), far(sketch), far(strain))


def eliminate(D, nb, w=8):
    groups = nb // 8
    W2 = 2 * nb
    ri = lax.broadcasted_iota(jnp.int32, (nb, nb), 0)
    ci = lax.broadcasted_iota(jnp.int32, (nb, nb), 1)
    eye = jnp.where(ri == ci, 1.0, 0.0).astype(f32)
    M = jnp.concatenate([D, eye], axis=1)
    Mv = [M[8 * k : 8 * k + 8, :] for k in range(groups)]
    sub = lax.broadcasted_iota(jnp.int32, (8, W2), 0)
    spread = lambda x: jnp.broadcast_to(x, (8, W2))
    for j in range(0, nb, w):
        g = j // 8
        a = [spread(Mv[(j + s) // 8][(j + s) % 8 : (j + s) % 8 + 1, :]) for s in range(w)]
        S = [
            [spread(a[s][:, j + t : j + t + 1]) if t >= s else None for t in range(w)]
            for s in range(w)
        ]
        c = {k: [spread(Mv[k][:, j + s : j + s + 1]) for s in range(w)] for k in range(g, groups)}
        inv = []
        for s in range(w):
            iv = 1.0 / S[s][s]
            inv.append(iv)
            for t in range(s + 1, w):
                f = S[s][t] * iv
                for u in range(t, w):
                    S[t][u] = S[t][u] - f * S[s][u]
                a[t] = a[t] - f * a[s]
        for k in range(g, groups):
            acc = Mv[k]
            for s in range(w):
                m = c[k][s] * inv[s]
                if k * 8 <= j + s:
                    m = jnp.where(sub + 8 * k > j + s, m, 0.0)
                acc = acc - m * a[s]
                for t in range(s + 1, w):
                    c[k][t] = c[k][t] - m * S[s][t]
            Mv[k] = acc
    M = jnp.concatenate(Mv, axis=0)
    diag = jnp.where(ri == ci, M[:, :nb], 0.0)
    d_col = jnp.sum(diag, axis=1, keepdims=True)
    d_row = jnp.sum(diag, axis=0, keepdims=True)
    return M[:, nb:] * lax.rsqrt(d_col), d_row * lax.rsqrt(d_row)


def basis_steps(product, scale, A, X, spec_ref):
    n, nb = product.shape[1], 128
    A[...] = dot(product, product, 0, 0, highest)
    X0, d0 = eliminate(A[:nb, :nb], nb)
    R = dot(X0, A[:nb, nb:], 1, 0, highest)
    X1, d1 = eliminate(A[nb:, nb:] - dot(R, R, 0, 0, highest), nb)
    X[:nb, :nb] = X0
    X[:nb, nb:] = jnp.zeros((nb, n - nb), f32)
    X[nb:, nb:] = X1
    X[nb:, :nb] = -dot(X1, dot(R, X0, 0, 0, highest), 1, 0, highest)
    spec_ref[...] = jnp.concatenate([d0, d1], axis=1) * scale
    return dot(product, X[...], 1, 1, highest).astype(bf16)


def basis_kernel(scale, p_ref, basis_ref, spec_ref, A, X):
    basis_ref[...] = basis_steps(p_ref[...], scale, A, X, spec_ref)


def strip_plan(tiles, length, levels, lead):
    plan, base = [], 0
    for r in range(levels):
        blocks = max(1, (length >> r) // LANES)
        rows = (tiles + lead) >> r
        held = (tiles >> r) + blocks - 1
        chunk = next(m for m in (17, 16, 8, 4, 2, 1) if held % m == 0 or (m == 17 and held > 17 and held % 17 >= 15))
        for d in range(2):
            plan.append((r, d, tiles >> r, blocks, rows, chunk, -(-held // chunk), base))
            base += -(-held // chunk) * chunk
    return plan, base


def decimate(rvs, x):
    n = LANES
    ri = lax.broadcasted_iota(jnp.int32, (n, n), 0)
    ci = lax.broadcasted_iota(jnp.int32, (n, n), 1)
    flip = jnp.where(ri + ci == n - 1, 1.0, 0.0).astype(f32)
    first = jnp.where(ri // 2 == ci, 1.0, 0.0).astype(f32)
    second = jnp.where(ri // 2 == ci - n // 2, 1.0, 0.0).astype(f32)
    rvs[0][...] = dot(x, flip, 1, 0, highest)
    for r in range(1, len(rvs)):
        count = rvs[r].shape[0]
        later = rvs[r - 1][pl.ds(1, count, stride=2), :]
        earlier = rvs[r - 1][pl.ds(0, count, stride=2), :]
        rvs[r][...] = (
            dot(later, first, 1, 0, highest) + dot(earlier, second, 1, 0, highest)
        ) * inv_root_two


def build_strip(entry, rv, strip):
    r, d, tiles, blocks, rows, chunk, count, base = entry
    n = LANES
    wide = chunk + 1
    span = (wide + 1) * n

    def step(i, carry):
        q = d * rows + rows - 1 - i * chunk
        z = jnp.concatenate(
            [rv[pl.ds(jnp.maximum(q - j, 0), 1), :] for j in range(wide + 1)], axis=1
        ).astype(bf16).astype(f32)
        z = jnp.broadcast_to(z, (16, span))
        z = pltpu.roll(z, span - 15, 1, stride=1, stride_axis=0)[:, : wide * n]
        at = pl.ds(pl.multiple_of((base + i * chunk) * n, n), chunk * n)
        for g in range(n // 16):
            k = n - 16 - 16 * g
            t = pltpu.roll(z, wide * n - k, 1) if k else z
            strip[16 * g : 16 * g + 16, at] = t[:, : chunk * n].astype(bf16)
        return carry

    lax.fori_loop(0, count, step, 0)


def filter_kernel(plan, levels, strip, basis_ref, *rest):
    outs, bwide, obufs, sems = (
        rest[:levels], rest[levels], rest[levels + 1 : 2 * levels + 1], rest[-1]
    )
    n = LANES
    length, width = basis_ref.shape
    for h in range(bwide.shape[0]):
        bwide[h] = basis_ref[:, h * n : (h + 1) * n].astype(f32)

    def every(taps, step):
        halves = [bwide[h, pl.ds(0, taps, stride=step), :] for h in range(bwide.shape[0])]
        return jnp.concatenate(halves, axis=1)

    for r, d, tiles, blocks, rows, chunk, count, base in plan:
        taps = length >> r
        if r == 0:
            weight = basis_ref[...]
        elif taps >= n:
            weight = every(taps, 1 << r).astype(bf16)
        else:
            weight = jnp.concatenate(
                [every(taps, 1 << r), jnp.zeros((n - taps, width), f32)], axis=0
            ).astype(bf16)
        group = min(32, tiles)
        span = group * n

        def tile(s, carry, r=r, d=d, tiles=tiles, blocks=blocks, base=base, group=group, span=span,
                 weight=weight):
            parts = []
            for t in range(group):
                p = base + tiles - 1 - (s * group + t)
                parts.append(strip[:, pl.ds(pl.multiple_of(p * n, n), blocks * n)])
            at = pl.ds(pl.multiple_of(s * span, span), span)
            obufs[r][d, at, :] = dot(jnp.concatenate(parts, axis=0), weight, 1, 0).astype(bf16)
            pltpu.make_async_copy(
                obufs[r].at[d, at, :], outs[r].at[0, d, at, :], sems.at[r]
            ).start()
            return carry

        lax.fori_loop(0, tiles // group, tile, 0)
    for r in range(levels):
        pltpu.make_async_copy(obufs[r], outs[r].at[0], sems.at[r]).wait()


def filters(plan, held, strip, basis, levels):
    length, width = basis.shape
    samples = plan[0][2] * LANES
    return pl.pallas_call(
        functools.partial(filter_kernel, plan, levels),
        out_shape=[
            jax.ShapeDtypeStruct((1, 2, samples >> r, width), bf16) for r in range(levels)
        ],
        in_specs=[pl.BlockSpec(memory_space=pltpu.VMEM)] * 2,
        out_specs=[pl.BlockSpec(memory_space=pl.ANY)] * levels,
        scratch_shapes=[pltpu.VMEM((width // LANES, length, LANES), f32)]
        + [pltpu.VMEM((2, samples >> r, width), bf16) for r in range(levels)]
        + [pltpu.SemaphoreType.DMA((levels,))],
        compiler_params=pltpu.CompilerParams(vmem_limit_bytes=40 << 20),
        cost_estimate=pl.CostEstimate(
            flops=2 * 2 * samples * length * width, bytes_accessed=26 << 20, transcendentals=0
        ),
        name="filters",
    )(strip, basis)


def mixing_kernel(bins, white_ref, bin_ref, *rest):
    bases, out_ref = rest[:bins], rest[bins]
    rows = white_ref.shape[0]
    white = white_ref[...]
    bin_col = jnp.transpose(jnp.broadcast_to(bin_ref[...], (8, rows)).astype(f32))[:, 0:1]
    acc = dot(white, bases[0][...], 1, 0)
    for k in range(1, bins):
        acc = jnp.where(bin_col == float(k), dot(white, bases[k][...], 1, 0), acc)
    out_ref[...] = acc.astype(bf16)


def local(bins, group_size, templates, owner_device, rate_code, rate_gains, sketch, strain):
    rows, length = templates.shape
    width = sketch.shape[1]
    levels = rate_gains.shape[0]
    lead = 16
    scale = 1.0 / (rows * group_size * math.sqrt(length))
    params = pltpu.CompilerParams(vmem_limit_bytes=24 << 20)
    plan, held = strip_plan(strain.shape[1] // LANES, length, levels, lead)
    white, product, strip, relative = products(
        bins, group_size, lead, plan, held, templates, owner_device.reshape(1, rows),
        rate_code.reshape(1, rows), rate_gains, sketch, strain,
    )
    basis, spectrum = pl.pallas_call(
        functools.partial(basis_kernel, scale),
        out_shape=[
            jax.ShapeDtypeStruct((length, width), bf16),
            jax.ShapeDtypeStruct((1, width), f32),
        ],
        scratch_shapes=[pltpu.VMEM((width, width), f32)] * 2,
        compiler_params=params,
        name="basis",
    )(product)
    others = [
        lax.ppermute(basis, "bin", [(i, (i - k) % bins) for i in range(bins)])
        for k in range(1, bins)
    ]
    filtered = filters(plan, held, strip, basis, levels)
    mixing = pl.pallas_call(
        functools.partial(mixing_kernel, bins),
        out_shape=jax.ShapeDtypeStruct((rows, width), bf16),
        compiler_params=params,
        name="mixing",
    )(white, relative, basis, *others)
    return (mixing, spectrum, *filtered)


def solution(mesh):
    return jax.shard_map(
        functools.partial(local, mesh.shape["bin"], mesh.shape["grp"]),
        mesh=mesh,
        in_specs=(
            P(("bin", "grp"), None),
            P(("bin", "grp"), None),
            P(("bin", "grp")),
            P(),
            P(),
            P(None, "grp"),
        ),
        out_specs=(P(("bin", "grp"), None), P("bin", None)) + (P("bin", None, "grp", None),) * 5,
        check_vma=False,
    )
```

```python
import functools
import math

import jax
import jax.numpy as jnp
from jax import lax
from jax.experimental import pallas as pl
from jax.experimental.pallas import tpu as pltpu
from jax.sharding import PartitionSpec as P

f32, bf16 = jnp.float32, jnp.bfloat16
highest = lax.Precision.HIGHEST
inv_root_two = 0.7071067811865476
LANES = 128


def dot(a, b, ca, cb, precision=None):
    return lax.dot_general(
        a, b, (((ca,), (cb,)), ((), ())), precision=precision, preferred_element_type=f32
    )


def split(x, parts):
    out = []
    for _ in range(parts):
        piece = x.astype(bf16)
        out.append(piece)
        x = x - piece.astype(f32)
    return out


def product_kernel(
    bins, group_size, planes, lead, plan, levels,
    t_hbm, owner_hbm, rate_hbm, gains_hbm, sketch_hbm, x_hbm,
    white_ref, product_ref, strip, bin_ref,
    t_ref, owner_ref, rate_ref, gains_ref, sketch_ref, x_ref, turned,
    halves, send1, recv1, send2, recv2, sendv, recvv, total, send3, recv3, sendy, recvy,
    full, edge, xe, *rest,
):
    rvs, in_sems, sems = rest[:levels], rest[levels], rest[levels + 1]
    rows, length = t_ref.shape
    half = length // 2
    part = half // planes // 2
    bin_at, at = lax.axis_index("bin"), lax.axis_index("grp")
    core, place = at & 1, at >> 1
    mesh_id = pl.DeviceIdType.MESH
    sibling = (bin_at, place * 2 + 1 - core)
    following = (bin_at, (at + 1) & (group_size - 1))
    leading = (bin_at, (at - 1) & (group_size - 1))

    def fellow(k):
        return ((place + k) & (planes - 1)) * 2 + core

    def other(k):
        return ((bin_at + k) & (bins - 1), at)

    loads = [
        pltpu.make_async_copy(src, dst, in_sems.at[i])
        for i, (src, dst) in enumerate(
            [
                (x_hbm, x_ref), (gains_hbm, gains_ref), (t_hbm, t_ref), (sketch_hbm, sketch_ref),
                (owner_hbm, owner_ref), (rate_hbm, rate_ref),
            ]
        )
    ]
    for load in loads:
        load.start()
    barrier = pltpu.get_barrier_semaphore()

    def greet(device):
        pl.semaphore_signal(barrier, inc=1, device_id=device, device_id_type=mesh_id)

    greet(sibling)
    greet(following)
    greet(leading)
    for k in range(1, bins):
        greet(other(k))

    @pl.loop(1, planes, unroll=True)
    def _(k):
        greet((bin_at, fellow(k)))

    def remote(src, dst, group, index, device):
        return pltpu.make_async_remote_copy(
            src_ref=src, dst_ref=dst, send_sem=sems.at[group, 0, index],
            recv_sem=sems.at[group, 1, index], device_id=device, device_id_type=mesh_id,
        )

    loads[1].wait()
    gains = jnp.concatenate(
        [gains_ref[...], jnp.zeros((8 - levels, length), f32)], axis=0
    )
    gains = jnp.concatenate(split(gains, 3), axis=0)
    loads[4].wait()
    loads[5].wait()
    shift = group_size.bit_length() - 1
    relative = ((owner_ref[...] >> shift) - bin_at) & (bins - 1)
    bin_ref[...] = relative
    bin_col = jnp.transpose(jnp.broadcast_to(relative, (8, rows)).astype(f32))[:, 0:1]
    rate = jnp.broadcast_to(rate_ref[...], (24, rows))
    which = lax.broadcasted_iota(jnp.int32, (24, rows), 0) % 8
    onehot = jnp.where(rate == which, 1.0, 0.0).astype(bf16)
    factor = dot(onehot, gains, 0, 0)
    loads[2].wait()
    white = (t_ref[...].astype(f32) * factor).astype(bf16)
    white_ref[...] = white
    turned[...] = jnp.transpose(white)
    loads[3].wait()
    sk = split(sketch_ref[...], 2)
    y = dot(white, sk[0], 1, 0) + dot(white, sk[1], 1, 0)
    width = y.shape[1]

    pl.semaphore_wait(barrier, planes + bins + 1)
    first = [remote(send1.at[k], recv1.at[k], 0, k, sibling) for k in range(bins)]
    second = [
        k and remote(send2.at[k], recv2.at[k], 1, k, other(k))
        for k in range(bins)
    ]
    across = [
        k and remote(sendy.at[k], recvy.at[k], 4, k, other(k))
        for k in range(bins)
    ]

    def spread(k):
        return remote(sendv.at[fellow(k) >> 1], recvv.at[k], 2, k, (bin_at, fellow(k)))

    def third(k):
        return remote(send3.at[fellow(k) >> 1], recv3.at[k], 3, k, (bin_at, fellow(k)))

    def fourth(k):
        mine = full.at[core, place]
        return remote(mine, mine, 5, k, (bin_at, fellow(k)))

    def hand(k):
        mine = full.at[core, (place - k) & (planes - 1)]
        return remote(mine, mine, 6, k, sibling)

    def form(k):
        pb = dot(turned[...], jnp.where(bin_col == float(k), y, 0.0).astype(bf16), 1, 0)
        halves[k, 0] = pb[:half]
        halves[k, 1] = pb[half:]
        send1[k] = halves[k, 1 - core].astype(bf16)
        first[k].start()

    def join(k):
        first[k].wait_recv()
        both = (halves[k, core] + recv1[k].astype(f32)).reshape(planes, 2, part, width)
        if k:
            send2[k] = both[:, 0].astype(bf16)
            second[k].start()
        else:
            total[...] = both[:, 0]
        sendv[:, k] = both[:, 1].astype(bf16)

    form(2)
    form(1)
    loads[0].wait()
    xrows = x_ref.shape[1] // LANES
    for d in range(2):
        for i in range(xrows):
            xe[pl.ds(d * (xrows + lead) + lead + i, 1), :] = x_ref[
                d : d + 1, i * LANES : (i + 1) * LANES
            ]
    edges = [
        remote(
            xe.at[pl.ds(d * (xrows + lead) + xrows, lead), :], edge.at[d], 4, bins + d, following
        )
        for d in range(2)
    ]
    for e in edges:
        e.start()
    join(2)
    form(3)
    join(1)
    form(0)
    join(3)
    join(0)

    @pl.loop(1, planes, unroll=True)
    def _(k):
        spread(k).start()

    for d in range(2):
        edges[d].wait_recv()
        xe[pl.ds(d * (xrows + lead), lead), :] = jnp.where(at > 0, edge[d], 0.0)
    decimate(rvs, xe[...])
    for entry in plan[:1]:
        build_strip(entry, rvs[entry[0]], strip)

    for k in range(1, bins):
        second[k].wait_recv()
        total[...] = total[...] + recv2[k].astype(f32)
    send3[...] = total[...].astype(bf16)

    @pl.loop(1, planes, unroll=True)
    def _(k):
        third(k).start()

    @pl.loop(1, planes, unroll=True)
    def _(k):
        spread(k).wait_recv()

    acc = sendv[place].astype(f32)
    for k in range(1, planes):
        acc = acc + recvv[k].astype(f32)
    for k in range(1, bins):
        sendy[k] = acc[k].astype(bf16)
        across[k].start()

    for entry in plan[1:2]:
        build_strip(entry, rvs[entry[0]], strip)

    @pl.loop(1, planes, unroll=True)
    def _(k):
        third(k).wait_recv()

    one = total[place]
    for k in range(1, planes):
        one = one + recv3[k].astype(f32)
    two = acc[0]
    for k in range(1, bins):
        across[k].wait_recv()
        two = two + recvy[k].astype(f32)
    full[core, place] = jnp.concatenate([one, two], axis=0)
    hand(0).start()

    @pl.loop(1, planes, unroll=True)
    def _(k):
        fourth(k).start()

    for entry in plan[2:]:
        build_strip(entry, rvs[entry[0]], strip)

    @pl.loop(1, planes, unroll=True)
    def _(k):
        fourth(k).wait_recv()
        hand(k).start()

    for d in range(2):
        edges[d].wait_send()
    for k in range(bins):
        first[k].wait_send()
    for k in range(1, bins):
        second[k].wait_send()
        across[k].wait_send()

    @pl.loop(1, planes, unroll=True)
    def _(k):
        spread(k).wait_send()
        third(k).wait_send()
        fourth(k).wait_send()

    @pl.loop(0, planes, unroll=True)
    def _(k):
        hand(k).wait()

    product_ref[...] = full[...].reshape(length, width)


def products(bins, group_size, lead, plan, held, templates, owner, rate, gains, sketch, strain):
    rows, length = templates.shape
    width = sketch.shape[1]
    levels = gains.shape[0]
    planes = group_size // 2
    half, part = length // 2, length // group_size // 2
    hbm = lambda: pl.BlockSpec(memory_space=pltpu.HBM)
    xrows = strain.shape[1] // LANES + lead
    vm = lambda: pl.BlockSpec(memory_space=pltpu.VMEM)
    far = lambda a: pltpu.with_memory_space_constraint(a, pltpu.HBM)
    return pl.pallas_call(
        functools.partial(product_kernel, bins, group_size, planes, lead, plan, levels),
        out_shape=[
            jax.ShapeDtypeStruct((rows, length), bf16),
            jax.ShapeDtypeStruct((length, width), f32),
            jax.ShapeDtypeStruct((LANES, held * LANES), bf16),
            jax.ShapeDtypeStruct((1, rows), jnp.int32),
        ],
        in_specs=[hbm() for _ in range(6)],
        out_specs=[vm() for _ in range(4)],
        scratch_shapes=[
            pltpu.VMEM(templates.shape, bf16),
            pltpu.VMEM(owner.shape, jnp.int32),
            pltpu.VMEM(rate.shape, jnp.int32),
            pltpu.VMEM(gains.shape, f32),
            pltpu.VMEM(sketch.shape, f32),
            pltpu.VMEM(strain.shape, f32),
            pltpu.VMEM((length, rows), bf16),
            pltpu.VMEM((bins, 2, half, width), f32),
            pltpu.VMEM((bins, half, width), bf16),
            pltpu.VMEM((bins, half, width), bf16),
            pltpu.VMEM((bins, planes, part, width), bf16),
            pltpu.VMEM((bins, planes, part, width), bf16),
            pltpu.VMEM((planes, bins, part, width), bf16),
            pltpu.VMEM((planes, bins, part, width), bf16),
            pltpu.VMEM((planes, part, width), f32),
            pltpu.VMEM((planes, part, width), bf16),
            pltpu.VMEM((planes, part, width), bf16),
            pltpu.VMEM((bins, part, width), bf16),
            pltpu.VMEM((bins, part, width), bf16),
            pltpu.VMEM((2, planes, 2 * part, width), f32),
            pltpu.VMEM((2, lead, LANES), f32),
            pltpu.VMEM((2 * xrows, LANES), f32),
        ]
        + [pltpu.VMEM((2 * xrows >> r, LANES), f32) for r in range(levels)]
        + [pltpu.SemaphoreType.DMA((6,)), pltpu.SemaphoreType.DMA((7, 2, planes))],
        compiler_params=pltpu.CompilerParams(
            vmem_limit_bytes=30 << 20, collective_id=0, has_side_effects=True
        ),
        name="products",
    )(far(templates), far(owner), far(rate), far(gains), far(sketch), far(strain))


def eliminate(D, nb):
    w, groups = 8, nb // 8
    ri = lax.broadcasted_iota(jnp.int32, (nb, nb), 0)
    ci = lax.broadcasted_iota(jnp.int32, (nb, nb), 1)
    eye = jnp.where(ri == ci, 1.0, 0.0).astype(f32)
    left = [D[8 * k : 8 * k + 8, :] for k in range(groups)]
    right = [eye[8 * k : 8 * k + 8, :] for k in range(groups)]
    sub = lax.broadcasted_iota(jnp.int32, (8, nb), 0)
    spread = lambda x: jnp.broadcast_to(x, (8, nb))
    for g in range(groups):
        j = g * w
        a = [spread(left[g][s : s + 1, :]) for s in range(w)]
        b = [spread(right[g][s : s + 1, :]) for s in range(w)]
        S = [
            [spread(a[s][:, j + t : j + t + 1]) if t >= s else None for t in range(w)]
            for s in range(w)
        ]
        inv = []
        for s in range(w):
            iv = 1.0 / S[s][s]
            inv.append(iv)
            for t in range(s + 1, w):
                f = S[s][t] * iv
                for u in range(t, w):
                    S[t][u] = S[t][u] - f * S[s][u]
                a[t] = a[t] - f * a[s]
                b[t] = b[t] - f * b[s]
        for k in range(g + 1, groups):
            c = [spread(left[k][:, j + s : j + s + 1]) for s in range(w)]
            lk, rk = left[k], right[k]
            for s in range(w):
                m = c[s] * inv[s]
                lk = lk - m * a[s]
                rk = rk - m * b[s]
                for t in range(s + 1, w):
                    c[t] = c[t] - m * S[s][t]
            left[k], right[k] = lk, rk
        l_own, r_own = a[0], b[0]
        for s in range(1, w):
            l_own = jnp.where(sub == s, a[s], l_own)
            r_own = jnp.where(sub == s, b[s], r_own)
        left[g], right[g] = l_own, r_own
    diag = jnp.where(ri == ci, jnp.concatenate(left, axis=0), 0.0)
    d_col = jnp.sum(diag, axis=1, keepdims=True)
    d_row = jnp.sum(diag, axis=0, keepdims=True)
    return jnp.concatenate(right, axis=0) * lax.rsqrt(d_col), d_row * lax.rsqrt(d_row)


def strip_plan(tiles, length, levels, lead):
    plan, base = [], 0
    for r in range(levels):
        blocks = max(1, (length >> r) // LANES)
        rows = (tiles + lead) >> r
        held = (tiles >> r) + blocks - 1
        chunk = next(m for m in (17, 16, 8, 4, 2, 1) if held % m == 0 or (m == 17 and held > 17 and held % 17 >= 15))
        for d in range(2):
            plan.append((r, d, tiles >> r, blocks, rows, chunk, -(-held // chunk), base))
            base += -(-held // chunk) * chunk
    return plan, base


def decimate(rvs, x):
    n = LANES
    ri = lax.broadcasted_iota(jnp.int32, (n, n), 0)
    ci = lax.broadcasted_iota(jnp.int32, (n, n), 1)
    flip = jnp.where(ri + ci == n - 1, 1.0, 0.0).astype(f32)
    first = jnp.where(ri // 2 == ci, 1.0, 0.0).astype(f32)
    second = jnp.where(ri // 2 == ci - n // 2, 1.0, 0.0).astype(f32)
    rvs[0][...] = dot(x, flip, 1, 0, highest)
    for r in range(1, len(rvs)):
        count = rvs[r].shape[0]
        later = rvs[r - 1][pl.ds(1, count, stride=2), :]
        earlier = rvs[r - 1][pl.ds(0, count, stride=2), :]
        rvs[r][...] = (
            dot(later, first, 1, 0, highest) + dot(earlier, second, 1, 0, highest)
        ) * inv_root_two


def build_strip(entry, rv, strip):
    r, d, tiles, blocks, rows, chunk, count, base = entry
    n = LANES
    wide = chunk + 1
    span = (wide + 1) * n

    def step(i, carry):
        q = d * rows + rows - 1 - i * chunk
        z = jnp.concatenate(
            [rv[pl.ds(jnp.maximum(q - j, 0), 1), :] for j in range(wide + 1)], axis=1
        ).astype(bf16).astype(f32)
        z = jnp.broadcast_to(z, (16, span))
        z = pltpu.roll(z, span - 15, 1, stride=1, stride_axis=0)[:, : wide * n]
        at = pl.ds(pl.multiple_of((base + i * chunk) * n, n), chunk * n)
        for g in range(n // 16):
            k = n - 16 - 16 * g
            t = pltpu.roll(z, wide * n - k, 1) if k else z
            strip[16 * g : 16 * g + 16, at] = t[:, : chunk * n].astype(bf16)
        return carry

    lax.fori_loop(0, count, step, 0)


def filter_level(entry, strip, weight, group, emit):
    r, d, tiles, blocks, rows, chunk, count, base = entry
    n = LANES
    group = min(group, tiles)
    span = group * n

    def tile(s, carry):
        parts = []
        for t in range(group):
            p = base + tiles - 1 - (s * group + t)
            parts.append(strip[:, pl.ds(pl.multiple_of(p * n, n), blocks * n)])
        at = pl.ds(pl.multiple_of(s * span, span), span)
        emit(at, dot(jnp.concatenate(parts, axis=0), weight, 1, 0).astype(bf16))
        return carry

    lax.fori_loop(0, tiles // group, tile, 0)


def finish_kernel(
    bins, scale, plan, levels, p_ref, white_ref, bin_ref, strip, basis_ref, spec_ref, mix_ref, *rest
):
    small, (A, bases, bwide, sems) = rest[: levels - 1], rest[levels - 1 :]
    length, width = p_ref.shape
    nb = width // 2
    bin_at, at = lax.axis_index("bin"), lax.axis_index("grp")
    mesh_id = pl.DeviceIdType.MESH

    def other(k):
        return ((bin_at + k) & (bins - 1), at)

    barrier = pltpu.get_barrier_semaphore()
    for k in range(1, bins):
        pl.semaphore_signal(barrier, inc=1, device_id=other(k), device_id_type=mesh_id)
    sends = [
        [
            pltpu.make_async_remote_copy(
                src_ref=bases.at[0, h], dst_ref=bases.at[bins - k, h],
                send_sem=sems.at[0, h, k], recv_sem=sems.at[1, h, k],
                device_id=other(k), device_id_type=mesh_id,
            )
            for k in range(1, bins)
        ]
        for h in range(2)
    ]
    p0 = p_ref[:, :nb]
    A[...] = dot(p_ref[...], p_ref[...], 0, 0, highest)
    x0, d0 = eliminate(A[:nb, :nb], nb)
    q0 = dot(p0, x0, 1, 1, highest)
    basis_ref[:, :nb] = q0.astype(bf16)
    bases[0, 0] = q0.astype(bf16)
    pl.semaphore_wait(barrier, bins - 1)
    for send in sends[0]:
        send.start()
    r01 = dot(x0, A[:nb, nb:], 1, 0, highest)
    left = p_ref[:, nb:] - dot(q0, r01, 1, 0, highest)
    x1, d1 = eliminate(A[nb:, nb:] - dot(r01, r01, 0, 0, highest), nb)
    q1 = dot(left, x1, 1, 1, highest)
    basis_ref[:, nb:] = q1.astype(bf16)
    bases[0, 1] = q1.astype(bf16)
    for send in sends[1]:
        send.start()
    spec_ref[...] = jnp.concatenate([d0, d1], axis=1) * scale
    n = LANES
    for h in range(bwide.shape[0]):
        bwide[h] = basis_ref[:, h * n : (h + 1) * n].astype(f32)
    for entry in plan[2:]:
        r, d = entry[:2]
        taps = length >> r
        weight = jnp.concatenate(
            [bwide[h, pl.ds(0, taps, stride=1 << r), :] for h in range(bwide.shape[0])], axis=1
        )
        if taps < n:
            weight = jnp.concatenate([weight, jnp.zeros((n - taps, width), f32)], axis=0)

        def emit(where, value, r=r, d=d):
            small[r - 1][d, where, :] = value

        filter_level(entry, strip, weight.astype(bf16), 16, emit)
    white = white_ref[...]
    rows = white.shape[0]
    bin_col = jnp.transpose(jnp.broadcast_to(bin_ref[...], (8, rows)).astype(f32))[:, 0:1]
    acc = dot(white, basis_ref[...], 1, 0)
    for h in range(2):
        for send in sends[h]:
            send.wait_recv()
    for k in range(1, bins):
        theirs = jnp.concatenate([bases[k, 0], bases[k, 1]], axis=1)
        acc = jnp.where(bin_col == float(k), dot(white, theirs, 1, 0), acc)
    mix_ref[...] = acc.astype(bf16)
    for h in range(2):
        for send in sends[h]:
            send.wait_send()


def finish(bins, scale, plan, levels, product, white, relative, strip):
    length, width = product.shape
    rows = white.shape[0]
    samples = plan[0][2] * LANES
    vm = lambda: pl.BlockSpec(memory_space=pltpu.VMEM)
    return pl.pallas_call(
        functools.partial(finish_kernel, bins, scale, plan, levels),
        out_shape=[
            jax.ShapeDtypeStruct((length, width), bf16),
            jax.ShapeDtypeStruct((1, width), f32),
            jax.ShapeDtypeStruct((rows, width), bf16),
        ]
        + [jax.ShapeDtypeStruct((2, samples >> r, width), bf16) for r in range(1, levels)],
        in_specs=[vm() for _ in range(4)],
        out_specs=[vm() for _ in range(levels + 2)],
        scratch_shapes=[
            pltpu.VMEM((width, width), f32),
            pltpu.VMEM((bins, 2, length, width // 2), bf16),
            pltpu.VMEM((width // LANES, length, LANES), f32),
            pltpu.SemaphoreType.DMA((2, 2, bins)),
        ],
        compiler_params=pltpu.CompilerParams(
            vmem_limit_bytes=24 << 20, collective_id=1, has_side_effects=True
        ),
        name="finish",
    )(product, white, relative, strip)


def output_kernel(plan, levels, strip, basis_ref, spec_ref, mix_ref, *rest):
    small, outs, held, sems = (
        rest[: levels - 1], rest[levels - 1 : 2 * levels + 1], rest[-2], rest[-1]
    )
    mix_out, spec_out, filtered = outs[0], outs[1], outs[2:]
    stores = [
        pltpu.make_async_copy(src, dst, sems.at[1 + i])
        for i, (src, dst) in enumerate(
            [(small[r - 1], filtered[r].at[0]) for r in range(1, levels)]
            + [(mix_ref, mix_out), (spec_ref, spec_out)]
        )
    ]
    for store in stores:
        store.start()
    weight = basis_ref[...]
    for entry in plan[:2]:
        d = entry[1]

        def emit(where, value, d=d):
            held[d, where, :] = value
            pltpu.make_async_copy(
                held.at[d, where, :], filtered[0].at[0, d, where, :], sems.at[0]
            ).start()

        filter_level(entry, strip, weight, 32, emit)
    pltpu.make_async_copy(held, filtered[0].at[0], sems.at[0]).wait()
    for store in stores:
        store.wait()


def output(plan, levels, strip, basis, spectrum, mixed, small):
    width = basis.shape[1]
    samples = plan[0][2] * LANES
    vm = lambda: pl.BlockSpec(memory_space=pltpu.VMEM)
    return pl.pallas_call(
        functools.partial(output_kernel, plan, levels),
        out_shape=[
            jax.ShapeDtypeStruct(mixed.shape, bf16),
            jax.ShapeDtypeStruct(spectrum.shape, f32),
        ]
        + [jax.ShapeDtypeStruct((1, 2, samples >> r, width), bf16) for r in range(levels)],
        in_specs=[vm() for _ in range(levels + 3)],
        out_specs=[pl.BlockSpec(memory_space=pl.ANY)] * (levels + 2),
        scratch_shapes=[
            pltpu.VMEM((2, samples, width), bf16),
            pltpu.SemaphoreType.DMA((levels + 2,)),
        ],
        compiler_params=pltpu.CompilerParams(vmem_limit_bytes=24 << 20),
        name="output",
    )(strip, basis, spectrum, mixed, *small)


def local(bins, group_size, templates, owner_device, rate_code, rate_gains, sketch, strain):
    rows, length = templates.shape
    levels = rate_gains.shape[0]
    lead = 16
    scale = 1.0 / (rows * group_size * math.sqrt(length))
    plan, held = strip_plan(strain.shape[1] // LANES, length, levels, lead)
    white, product, strip, relative = products(
        bins, group_size, lead, plan, held, templates, owner_device.reshape(1, rows),
        rate_code.reshape(1, rows), rate_gains, sketch, strain,
    )
    basis, spectrum, mixed, *small = finish(
        bins, scale, plan, levels, product, white, relative, strip
    )
    return tuple(output(plan, levels, strip, basis, spectrum, mixed, small))


def solution(mesh):
    return jax.shard_map(
        functools.partial(local, mesh.shape["bin"], mesh.shape["grp"]),
        mesh=mesh,
        in_specs=(
            P(("bin", "grp"), None),
            P(("bin", "grp"), None),
            P(("bin", "grp")),
            P(),
            P(),
            P(None, "grp"),
        ),
        out_specs=(P(("bin", "grp"), None), P("bin", None)) + (P("bin", None, "grp", None),) * 5,
        check_vma=False,
    )
```

```python
import functools
import math

import jax
import jax.numpy as jnp
from jax import lax
from jax.experimental import pallas as pl
from jax.experimental.pallas import tpu as pltpu
from jax.sharding import PartitionSpec as P

f32, bf16 = jnp.float32, jnp.bfloat16
highest = lax.Precision.HIGHEST
inv_root_two = 0.7071067811865476
LANES = 128


def dot(a, b, ca, cb, precision=None):
    return lax.dot_general(
        a, b, (((ca,), (cb,)), ((), ())), precision=precision, preferred_element_type=f32
    )


def at_once(start):
    @pl.when(lax.axis_index("grp") >= 0)
    def _():
        start()


def split(x, parts):
    out = []
    for _ in range(parts):
        piece = x.astype(bf16)
        out.append(piece)
        x = x - piece.astype(f32)
    return out


def product_kernel(
    bins, group_size, planes, lead, plan, levels,
    t_hbm, owner_hbm, rate_hbm, gains_hbm, sketch_hbm, x_hbm,
    white_ref, product_ref, strip, bin_ref,
    t_ref, owner_ref, rate_ref, gains_ref, sketch_ref, x_ref, turned,
    halves, send1, recv1, send2, recv2, sendv, recvv, total, send3, recv3, sendy, recvy,
    full, edge, xe, *rest,
):
    rvs, in_sems, sems = rest[:levels], rest[levels], rest[levels + 1]
    rows, length = t_ref.shape
    half = length // 2
    part = half // planes // 2
    bin_at, at = lax.axis_index("bin"), lax.axis_index("grp")
    core, place = at & 1, at >> 1
    mesh_id = pl.DeviceIdType.MESH
    sibling = (bin_at, place * 2 + 1 - core)
    following = (bin_at, (at + 1) & (group_size - 1))
    leading = (bin_at, (at - 1) & (group_size - 1))

    def fellow(k):
        return ((place + k) & (planes - 1)) * 2 + core

    def other(k):
        return ((bin_at + k) & (bins - 1), at)

    loads = [
        pltpu.make_async_copy(src, dst, in_sems.at[i])
        for i, (src, dst) in enumerate(
            [
                (x_hbm, x_ref), (gains_hbm, gains_ref), (t_hbm, t_ref), (sketch_hbm, sketch_ref),
                (owner_hbm, owner_ref), (rate_hbm, rate_ref),
            ]
        )
    ]
    for load in loads:
        load.start()
    barrier = pltpu.get_barrier_semaphore()

    def greet(device):
        pl.semaphore_signal(barrier, inc=1, device_id=device, device_id_type=mesh_id)

    greet(sibling)
    greet(following)
    greet(leading)
    for k in range(1, bins):
        greet(other(k))

    @pl.loop(1, planes, unroll=True)
    def _(k):
        greet((bin_at, fellow(k)))

    def remote(src, dst, group, index, device):
        return pltpu.make_async_remote_copy(
            src_ref=src, dst_ref=dst, send_sem=sems.at[group, 0, index],
            recv_sem=sems.at[group, 1, index], device_id=device, device_id_type=mesh_id,
        )

    loads[1].wait()
    gains = jnp.concatenate(
        [gains_ref[...], jnp.zeros((8 - levels, length), f32)], axis=0
    )
    gains = jnp.concatenate(split(gains, 3), axis=0)
    loads[4].wait()
    loads[5].wait()
    shift = group_size.bit_length() - 1
    relative = ((owner_ref[...] >> shift) - bin_at) & (bins - 1)
    bin_ref[...] = relative
    bin_col = jnp.transpose(jnp.broadcast_to(relative, (8, rows)).astype(f32))[:, 0:1]
    rate = jnp.broadcast_to(rate_ref[...], (24, rows))
    which = lax.broadcasted_iota(jnp.int32, (24, rows), 0) % 8
    onehot = jnp.where(rate == which, 1.0, 0.0).astype(bf16)
    factor = dot(onehot, gains, 0, 0)
    loads[2].wait()
    white = (t_ref[...].astype(f32) * factor).astype(bf16)
    white_ref[...] = white
    turned[...] = jnp.transpose(white)
    loads[3].wait()
    sk = split(sketch_ref[...], 2)
    y = dot(white, sk[0], 1, 0) + dot(white, sk[1], 1, 0)
    width = y.shape[1]

    pl.semaphore_wait(barrier, planes + bins + 1)
    first = [remote(send1.at[k], recv1.at[k], 0, k, sibling) for k in range(bins)]
    second = [
        k and remote(send2.at[k], recv2.at[k], 1, k, other(k))
        for k in range(bins)
    ]
    across = [
        k and remote(sendy.at[k], recvy.at[k], 4, k, other(k))
        for k in range(bins)
    ]

    def spread(k):
        return remote(sendv.at[fellow(k) >> 1], recvv.at[k], 2, k, (bin_at, fellow(k)))

    def third(k):
        return remote(send3.at[fellow(k) >> 1], recv3.at[k], 3, k, (bin_at, fellow(k)))

    def fourth(k):
        mine = full.at[core, place]
        return remote(mine, mine, 5, k, (bin_at, fellow(k)))

    def hand(k):
        mine = full.at[core, (place - k) & (planes - 1)]
        return remote(mine, mine, 6, k, sibling)

    def form(k):
        pb = dot(turned[...], jnp.where(bin_col == float(k), y, 0.0).astype(bf16), 1, 0)
        halves[k, 0] = pb[:half]
        halves[k, 1] = pb[half:]
        send1[k] = halves[k, 1 - core].astype(bf16)
        at_once(lambda: first[k].start())

    def join(k):
        first[k].wait_recv()
        both = (halves[k, core] + recv1[k].astype(f32)).reshape(planes, 2, part, width)
        if k:
            send2[k] = both[:, 0].astype(bf16)
            at_once(lambda: second[k].start())
        else:
            total[...] = both[:, 0]
        sendv[:, k] = both[:, 1].astype(bf16)

    form(2)
    form(1)
    loads[0].wait()
    xrows = x_ref.shape[1] // LANES
    for d in range(2):
        for i in range(xrows):
            xe[pl.ds(d * (xrows + lead) + lead + i, 1), :] = x_ref[
                d : d + 1, i * LANES : (i + 1) * LANES
            ]
    edges = [
        remote(
            xe.at[pl.ds(d * (xrows + lead) + xrows, lead), :], edge.at[d], 4, bins + d, following
        )
        for d in range(2)
    ]
    at_once(lambda: [e.start() for e in edges])
    join(2)
    form(3)
    join(1)
    form(0)
    join(3)
    join(0)

    @pl.loop(1, planes, unroll=True)
    def _(k):
        spread(k).start()

    for d in range(2):
        edges[d].wait_recv()
        xe[pl.ds(d * (xrows + lead), lead), :] = jnp.where(at > 0, edge[d], 0.0)
    decimate(rvs, xe[...])
    for entry in plan[:1]:
        build_strip(entry, rvs[entry[0]], strip)

    for k in range(1, bins):
        second[k].wait_recv()
        total[...] = total[...] + recv2[k].astype(f32)
    send3[...] = total[...].astype(bf16)

    @pl.loop(1, planes, unroll=True)
    def _(k):
        third(k).start()

    @pl.loop(1, planes, unroll=True)
    def _(k):
        spread(k).wait_recv()

    acc = sendv[place].astype(f32)
    for k in range(1, planes):
        acc = acc + recvv[k].astype(f32)
    for k in range(1, bins):
        sendy[k] = acc[k].astype(bf16)
        at_once(lambda: across[k].start())

    for entry in plan[1:2]:
        build_strip(entry, rvs[entry[0]], strip)

    @pl.loop(1, planes, unroll=True)
    def _(k):
        third(k).wait_recv()

    one = total[place]
    for k in range(1, planes):
        one = one + recv3[k].astype(f32)
    two = acc[0]
    for k in range(1, bins):
        across[k].wait_recv()
        two = two + recvy[k].astype(f32)
    full[core, place] = jnp.concatenate([one, two], axis=0)
    hand(0).start()

    @pl.loop(1, planes, unroll=True)
    def _(k):
        fourth(k).start()

    for entry in plan[2:]:
        build_strip(entry, rvs[entry[0]], strip)

    @pl.loop(1, planes, unroll=True)
    def _(k):
        fourth(k).wait_recv()
        hand(k).start()

    for d in range(2):
        edges[d].wait_send()
    for k in range(bins):
        first[k].wait_send()
    for k in range(1, bins):
        second[k].wait_send()
        across[k].wait_send()

    @pl.loop(1, planes, unroll=True)
    def _(k):
        spread(k).wait_send()
        third(k).wait_send()
        fourth(k).wait_send()

    @pl.loop(0, planes, unroll=True)
    def _(k):
        hand(k).wait()

    product_ref[...] = full[...].reshape(length, width)


def products(bins, group_size, lead, plan, held, templates, owner, rate, gains, sketch, strain):
    rows, length = templates.shape
    width = sketch.shape[1]
    levels = gains.shape[0]
    planes = group_size // 2
    half, part = length // 2, length // group_size // 2
    hbm = lambda: pl.BlockSpec(memory_space=pltpu.HBM)
    xrows = strain.shape[1] // LANES + lead
    vm = lambda: pl.BlockSpec(memory_space=pltpu.VMEM)
    far = lambda a: pltpu.with_memory_space_constraint(a, pltpu.HBM)
    return pl.pallas_call(
        functools.partial(product_kernel, bins, group_size, planes, lead, plan, levels),
        out_shape=[
            jax.ShapeDtypeStruct((rows, length), bf16),
            jax.ShapeDtypeStruct((length, width), f32),
            jax.ShapeDtypeStruct((LANES, held * LANES), bf16),
            jax.ShapeDtypeStruct((1, rows), jnp.int32),
        ],
        in_specs=[hbm() for _ in range(6)],
        out_specs=[vm() for _ in range(4)],
        scratch_shapes=[
            pltpu.VMEM(templates.shape, bf16),
            pltpu.VMEM(owner.shape, jnp.int32),
            pltpu.VMEM(rate.shape, jnp.int32),
            pltpu.VMEM(gains.shape, f32),
            pltpu.VMEM(sketch.shape, f32),
            pltpu.VMEM(strain.shape, f32),
            pltpu.VMEM((length, rows), bf16),
            pltpu.VMEM((bins, 2, half, width), f32),
            pltpu.VMEM((bins, half, width), bf16),
            pltpu.VMEM((bins, half, width), bf16),
            pltpu.VMEM((bins, planes, part, width), bf16),
            pltpu.VMEM((bins, planes, part, width), bf16),
            pltpu.VMEM((planes, bins, part, width), bf16),
            pltpu.VMEM((planes, bins, part, width), bf16),
            pltpu.VMEM((planes, part, width), f32),
            pltpu.VMEM((planes, part, width), bf16),
            pltpu.VMEM((planes, part, width), bf16),
            pltpu.VMEM((bins, part, width), bf16),
            pltpu.VMEM((bins, part, width), bf16),
            pltpu.VMEM((2, planes, 2 * part, width), f32),
            pltpu.VMEM((2, lead, LANES), f32),
            pltpu.VMEM((2 * xrows, LANES), f32),
        ]
        + [pltpu.VMEM((2 * xrows >> r, LANES), f32) for r in range(levels)]
        + [pltpu.SemaphoreType.DMA((6,)), pltpu.SemaphoreType.DMA((7, 2, planes))],
        compiler_params=pltpu.CompilerParams(
            vmem_limit_bytes=30 << 20, collective_id=0, has_side_effects=True
        ),
        name="products",
    )(far(templates), far(owner), far(rate), far(gains), far(sketch), far(strain))


def eliminate(D, nb):
    w, groups = 8, nb // 8
    ri = lax.broadcasted_iota(jnp.int32, (nb, nb), 0)
    ci = lax.broadcasted_iota(jnp.int32, (nb, nb), 1)
    eye = jnp.where(ri == ci, 1.0, 0.0).astype(f32)
    left = [D[8 * k : 8 * k + 8, :] for k in range(groups)]
    right = [eye[8 * k : 8 * k + 8, :] for k in range(groups)]
    sub = lax.broadcasted_iota(jnp.int32, (8, nb), 0)
    spread = lambda x: jnp.broadcast_to(x, (8, nb))
    for g in range(groups):
        j = g * w
        a = [spread(left[g][s : s + 1, :]) for s in range(w)]
        b = [spread(right[g][s : s + 1, :]) for s in range(w)]
        S = [
            [spread(a[s][:, j + t : j + t + 1]) if t >= s else None for t in range(w)]
            for s in range(w)
        ]
        inv = []
        for s in range(w):
            iv = 1.0 / S[s][s]
            inv.append(iv)
            for t in range(s + 1, w):
                f = S[s][t] * iv
                for u in range(t, w):
                    S[t][u] = S[t][u] - f * S[s][u]
                a[t] = a[t] - f * a[s]
                b[t] = b[t] - f * b[s]
        for k in range(g + 1, groups):
            c = [spread(left[k][:, j + s : j + s + 1]) for s in range(w)]
            lk, rk = left[k], right[k]
            for s in range(w):
                m = c[s] * inv[s]
                lk = lk - m * a[s]
                rk = rk - m * b[s]
                for t in range(s + 1, w):
                    c[t] = c[t] - m * S[s][t]
            left[k], right[k] = lk, rk
        l_own, r_own = a[0], b[0]
        for s in range(1, w):
            l_own = jnp.where(sub == s, a[s], l_own)
            r_own = jnp.where(sub == s, b[s], r_own)
        left[g], right[g] = l_own, r_own
    diag = jnp.where(ri == ci, jnp.concatenate(left, axis=0), 0.0)
    d_col = jnp.sum(diag, axis=1, keepdims=True)
    d_row = jnp.sum(diag, axis=0, keepdims=True)
    return jnp.concatenate(right, axis=0) * lax.rsqrt(d_col), d_row * lax.rsqrt(d_row)


def strip_plan(tiles, length, levels, lead):
    plan, base = [], 0
    for r in range(levels):
        blocks = max(1, (length >> r) // LANES)
        rows = (tiles + lead) >> r
        held = (tiles >> r) + blocks - 1
        chunk = next(m for m in (17, 16, 8, 4, 2, 1) if held % m == 0 or (m == 17 and held > 17 and held % 17 >= 15))
        for d in range(2):
            plan.append((r, d, tiles >> r, blocks, rows, chunk, -(-held // chunk), base))
            base += -(-held // chunk) * chunk
    return plan, base


def decimate(rvs, x):
    n = LANES
    ri = lax.broadcasted_iota(jnp.int32, (n, n), 0)
    ci = lax.broadcasted_iota(jnp.int32, (n, n), 1)
    flip = jnp.where(ri + ci == n - 1, 1.0, 0.0).astype(f32)
    first = jnp.where(ri // 2 == ci, 1.0, 0.0).astype(f32)
    second = jnp.where(ri // 2 == ci - n // 2, 1.0, 0.0).astype(f32)
    rvs[0][...] = dot(x, flip, 1, 0, highest)
    for r in range(1, len(rvs)):
        count = rvs[r].shape[0]
        later = rvs[r - 1][pl.ds(1, count, stride=2), :]
        earlier = rvs[r - 1][pl.ds(0, count, stride=2), :]
        rvs[r][...] = (
            dot(later, first, 1, 0, highest) + dot(earlier, second, 1, 0, highest)
        ) * inv_root_two


def build_strip(entry, rv, strip):
    r, d, tiles, blocks, rows, chunk, count, base = entry
    n = LANES
    wide = chunk + 1
    span = (wide + 1) * n

    def step(i, carry):
        q = d * rows + rows - 1 - i * chunk
        z = jnp.concatenate(
            [rv[pl.ds(jnp.maximum(q - j, 0), 1), :] for j in range(wide + 1)], axis=1
        ).astype(bf16).astype(f32)
        z = jnp.broadcast_to(z, (16, span))
        z = pltpu.roll(z, span - 15, 1, stride=1, stride_axis=0)[:, : wide * n]
        at = pl.ds(pl.multiple_of((base + i * chunk) * n, n), chunk * n)
        for g in range(n // 16):
            k = n - 16 - 16 * g
            t = pltpu.roll(z, wide * n - k, 1) if k else z
            strip[16 * g : 16 * g + 16, at] = t[:, : chunk * n].astype(bf16)
        return carry

    lax.fori_loop(0, count, step, 0)


def filter_level(entry, strip, weight, group, emit):
    r, d, tiles, blocks, rows, chunk, count, base = entry
    n = LANES
    group = min(group, tiles)
    span = group * n

    def tile(s, carry):
        parts = []
        for t in range(group):
            p = base + tiles - 1 - (s * group + t)
            parts.append(strip[:, pl.ds(pl.multiple_of(p * n, n), blocks * n)])
        at = pl.ds(pl.multiple_of(s * span, span), span)
        emit(at, dot(jnp.concatenate(parts, axis=0), weight, 1, 0).astype(bf16))
        return carry

    lax.fori_loop(0, tiles // group, tile, 0)


def finish_kernel(
    bins, scale, plan, levels, p_ref, white_ref, bin_ref, strip, basis_ref, spec_ref, mix_ref, *rest
):
    small, (A, bases, bwide, sems) = rest[: levels - 1], rest[levels - 1 :]
    length, width = p_ref.shape
    nb = width // 2
    bin_at, at = lax.axis_index("bin"), lax.axis_index("grp")
    mesh_id = pl.DeviceIdType.MESH

    def other(k):
        return ((bin_at + k) & (bins - 1), at)

    barrier = pltpu.get_barrier_semaphore()
    for k in range(1, bins):
        pl.semaphore_signal(barrier, inc=1, device_id=other(k), device_id_type=mesh_id)
    sends = [
        [
            pltpu.make_async_remote_copy(
                src_ref=bases.at[0, h], dst_ref=bases.at[bins - k, h],
                send_sem=sems.at[0, h, k], recv_sem=sems.at[1, h, k],
                device_id=other(k), device_id_type=mesh_id,
            )
            for k in range(1, bins)
        ]
        for h in range(2)
    ]
    p0 = p_ref[:, :nb]
    A[...] = dot(p_ref[...], p_ref[...], 0, 0, highest)
    x0, d0 = eliminate(A[:nb, :nb], nb)
    q0 = dot(p0, x0, 1, 1, highest)
    basis_ref[:, :nb] = q0.astype(bf16)
    bases[0, 0] = q0.astype(bf16)
    pl.semaphore_wait(barrier, bins - 1)
    at_once(lambda: [send.start() for send in sends[0]])
    r01 = dot(x0, A[:nb, nb:], 1, 0, highest)
    left = p_ref[:, nb:] - dot(q0, r01, 1, 0, highest)
    x1, d1 = eliminate(A[nb:, nb:] - dot(r01, r01, 0, 0, highest), nb)
    q1 = dot(left, x1, 1, 1, highest)
    basis_ref[:, nb:] = q1.astype(bf16)
    bases[0, 1] = q1.astype(bf16)
    at_once(lambda: [send.start() for send in sends[1]])
    spec_ref[...] = jnp.concatenate([d0, d1], axis=1) * scale
    n = LANES
    for h in range(bwide.shape[0]):
        bwide[h] = basis_ref[:, h * n : (h + 1) * n].astype(f32)
    for entry in plan[2:]:
        r, d = entry[:2]
        taps = length >> r
        weight = jnp.concatenate(
            [bwide[h, pl.ds(0, taps, stride=1 << r), :] for h in range(bwide.shape[0])], axis=1
        )
        if taps < n:
            weight = jnp.concatenate([weight, jnp.zeros((n - taps, width), f32)], axis=0)

        def emit(where, value, r=r, d=d):
            small[r - 1][d, where, :] = value

        filter_level(entry, strip, weight.astype(bf16), 16, emit)
    white = white_ref[...]
    rows = white.shape[0]
    bin_col = jnp.transpose(jnp.broadcast_to(bin_ref[...], (8, rows)).astype(f32))[:, 0:1]
    acc = dot(white, basis_ref[...], 1, 0)
    for h in range(2):
        for send in sends[h]:
            send.wait_recv()
    for k in range(1, bins):
        theirs = jnp.concatenate([bases[k, 0], bases[k, 1]], axis=1)
        acc = jnp.where(bin_col == float(k), dot(white, theirs, 1, 0), acc)
    mix_ref[...] = acc.astype(bf16)
    for h in range(2):
        for send in sends[h]:
            send.wait_send()


def finish(bins, scale, plan, levels, product, white, relative, strip):
    length, width = product.shape
    rows = white.shape[0]
    samples = plan[0][2] * LANES
    vm = lambda: pl.BlockSpec(memory_space=pltpu.VMEM)
    return pl.pallas_call(
        functools.partial(finish_kernel, bins, scale, plan, levels),
        out_shape=[
            jax.ShapeDtypeStruct((length, width), bf16),
            jax.ShapeDtypeStruct((1, width), f32),
            jax.ShapeDtypeStruct((rows, width), bf16),
        ]
        + [jax.ShapeDtypeStruct((2, samples >> r, width), bf16) for r in range(1, levels)],
        in_specs=[vm() for _ in range(4)],
        out_specs=[vm() for _ in range(levels + 2)],
        scratch_shapes=[
            pltpu.VMEM((width, width), f32),
            pltpu.VMEM((bins, 2, length, width // 2), bf16),
            pltpu.VMEM((width // LANES, length, LANES), f32),
            pltpu.SemaphoreType.DMA((2, 2, bins)),
        ],
        compiler_params=pltpu.CompilerParams(
            vmem_limit_bytes=24 << 20, collective_id=1, has_side_effects=True
        ),
        name="finish",
    )(product, white, relative, strip)


def output_kernel(plan, levels, strip, basis_ref, spec_ref, mix_ref, *rest):
    small, outs, held, sems = (
        rest[: levels - 1], rest[levels - 1 : 2 * levels + 1], rest[-2], rest[-1]
    )
    mix_out, spec_out, filtered = outs[0], outs[1], outs[2:]
    stores = [
        pltpu.make_async_copy(src, dst, sems.at[1 + i])
        for i, (src, dst) in enumerate(
            [(small[r - 1], filtered[r].at[0]) for r in range(1, levels)]
            + [(mix_ref, mix_out), (spec_ref, spec_out)]
        )
    ]
    for store in stores:
        store.start()
    weight = basis_ref[...]
    for entry in plan[:2]:
        d = entry[1]

        def emit(where, value, d=d):
            held[d, where, :] = value
            pltpu.make_async_copy(
                held.at[d, where, :], filtered[0].at[0, d, where, :], sems.at[0]
            ).start()

        filter_level(entry, strip, weight, 32, emit)
    pltpu.make_async_copy(held, filtered[0].at[0], sems.at[0]).wait()
    for store in stores:
        store.wait()


def output(plan, levels, strip, basis, spectrum, mixed, small):
    width = basis.shape[1]
    samples = plan[0][2] * LANES
    vm = lambda: pl.BlockSpec(memory_space=pltpu.VMEM)
    return pl.pallas_call(
        functools.partial(output_kernel, plan, levels),
        out_shape=[
            jax.ShapeDtypeStruct(mixed.shape, bf16),
            jax.ShapeDtypeStruct(spectrum.shape, f32),
        ]
        + [jax.ShapeDtypeStruct((1, 2, samples >> r, width), bf16) for r in range(levels)],
        in_specs=[vm() for _ in range(levels + 3)],
        out_specs=[pl.BlockSpec(memory_space=pl.ANY)] * (levels + 2),
        scratch_shapes=[
            pltpu.VMEM((2, samples, width), bf16),
            pltpu.SemaphoreType.DMA((levels + 2,)),
        ],
        compiler_params=pltpu.CompilerParams(vmem_limit_bytes=24 << 20),
        name="output",
    )(strip, basis, spectrum, mixed, *small)


def local(bins, group_size, templates, owner_device, rate_code, rate_gains, sketch, strain):
    rows, length = templates.shape
    levels = rate_gains.shape[0]
    lead = 16
    scale = 1.0 / (rows * group_size * math.sqrt(length))
    plan, held = strip_plan(strain.shape[1] // LANES, length, levels, lead)
    white, product, strip, relative = products(
        bins, group_size, lead, plan, held, templates, owner_device.reshape(1, rows),
        rate_code.reshape(1, rows), rate_gains, sketch, strain,
    )
    basis, spectrum, mixed, *small = finish(
        bins, scale, plan, levels, product, white, relative, strip
    )
    return tuple(output(plan, levels, strip, basis, spectrum, mixed, small))


def solution(mesh):
    return jax.shard_map(
        functools.partial(local, mesh.shape["bin"], mesh.shape["grp"]),
        mesh=mesh,
        in_specs=(
            P(("bin", "grp"), None),
            P(("bin", "grp"), None),
            P(("bin", "grp")),
            P(),
            P(),
            P(None, "grp"),
        ),
        out_specs=(P(("bin", "grp"), None), P("bin", None)) + (P("bin", None, "grp", None),) * 5,
        check_vma=False,
    )
```

```python
import functools
import math

import jax
import jax.numpy as jnp
from jax import lax
from jax.experimental import pallas as pl
from jax.experimental.pallas import tpu as pltpu
from jax.sharding import PartitionSpec as P

f32, bf16 = jnp.float32, jnp.bfloat16
highest = lax.Precision.HIGHEST
inv_root_two = 0.7071067811865476
LANES = 128


def dot(a, b, ca, cb, precision=None):
    return lax.dot_general(
        a, b, (((ca,), (cb,)), ((), ())), precision=precision, preferred_element_type=f32
    )


def at_once(start):
    @pl.when(lax.axis_index("grp") >= 0)
    def _():
        start()


def split(x, parts):
    out = []
    for _ in range(parts):
        piece = x.astype(bf16)
        out.append(piece)
        x = x - piece.astype(f32)
    return out


def product_kernel(
    bins, group_size, planes, lead, plan, levels,
    t_hbm, owner_hbm, rate_hbm, gains_hbm, sketch_hbm, x_hbm,
    white_ref, product_ref, strip, bin_ref,
    t_ref, owner_ref, rate_ref, gains_ref, sketch_ref, x_ref, turned,
    halves, send1, recv1, send2, recv2, sendv, recvv, total, send3, recv3, sendy, recvy,
    full, edge, xe, *rest,
):
    rvs, in_sems, sems = rest[:levels], rest[levels], rest[levels + 1]
    rows, length = t_ref.shape
    half = length // 2
    part = half // planes // 2
    bin_at, at = lax.axis_index("bin"), lax.axis_index("grp")
    core, place = at & 1, at >> 1
    mesh_id = pl.DeviceIdType.MESH
    sibling = (bin_at, place * 2 + 1 - core)
    following = (bin_at, (at + 1) & (group_size - 1))
    leading = (bin_at, (at - 1) & (group_size - 1))

    def fellow(k):
        return ((place + k) & (planes - 1)) * 2 + core

    def other(k):
        return ((bin_at + k) & (bins - 1), at)

    loads = [
        pltpu.make_async_copy(src, dst, in_sems.at[i])
        for i, (src, dst) in enumerate(
            [
                (x_hbm, x_ref), (gains_hbm, gains_ref), (t_hbm, t_ref), (sketch_hbm, sketch_ref),
                (owner_hbm, owner_ref), (rate_hbm, rate_ref),
            ]
        )
    ]
    for load in loads:
        load.start()
    barrier = pltpu.get_barrier_semaphore()

    def greet(device):
        pl.semaphore_signal(barrier, inc=1, device_id=device, device_id_type=mesh_id)

    greet(sibling)
    greet(following)
    greet(leading)
    for k in range(1, bins):
        greet(other(k))

    @pl.loop(1, planes, unroll=True)
    def _(k):
        greet((bin_at, fellow(k)))

    def remote(src, dst, group, index, device):
        return pltpu.make_async_remote_copy(
            src_ref=src, dst_ref=dst, send_sem=sems.at[group, 0, index],
            recv_sem=sems.at[group, 1, index], device_id=device, device_id_type=mesh_id,
        )

    loads[1].wait()
    gains = jnp.concatenate(
        [gains_ref[...], jnp.zeros((8 - levels, length), f32)], axis=0
    )
    gains = jnp.concatenate(split(gains, 3), axis=0)
    loads[4].wait()
    loads[5].wait()
    shift = group_size.bit_length() - 1
    relative = ((owner_ref[...] >> shift) - bin_at) & (bins - 1)
    bin_ref[...] = relative
    bin_col = jnp.transpose(jnp.broadcast_to(relative, (8, rows)).astype(f32))[:, 0:1]
    rate = jnp.broadcast_to(rate_ref[...], (24, rows))
    which = lax.broadcasted_iota(jnp.int32, (24, rows), 0) % 8
    onehot = jnp.where(rate == which, 1.0, 0.0).astype(bf16)
    factor = dot(onehot, gains, 0, 0)
    loads[2].wait()
    white = (t_ref[...].astype(f32) * factor).astype(bf16)
    white_ref[...] = white
    turned[...] = jnp.transpose(white)
    loads[3].wait()
    sk = split(sketch_ref[...], 2)
    y = dot(white, sk[0], 1, 0) + dot(white, sk[1], 1, 0)
    width = y.shape[1]

    pl.semaphore_wait(barrier, planes + bins + 1)
    first = [remote(send1.at[k], recv1.at[k], 0, k, sibling) for k in range(bins)]
    second = [
        k and remote(send2.at[k], recv2.at[k], 1, k, other(k))
        for k in range(bins)
    ]
    across = [
        k and remote(sendy.at[k], recvy.at[k], 4, k, other(k))
        for k in range(bins)
    ]

    def spread(k):
        return remote(sendv.at[fellow(k) >> 1], recvv.at[k], 2, k, (bin_at, fellow(k)))

    def third(k):
        return remote(send3.at[fellow(k) >> 1], recv3.at[k], 3, k, (bin_at, fellow(k)))

    def fourth(k):
        mine = full.at[core, place]
        return remote(mine, mine, 5, k, (bin_at, fellow(k)))

    def hand(k):
        mine = full.at[core, (place - k) & (planes - 1)]
        return remote(mine, mine, 6, k, sibling)

    def form(k):
        pb = dot(turned[...], jnp.where(bin_col == float(k), y, 0.0).astype(bf16), 1, 0)
        halves[k, 0] = pb[:half]
        halves[k, 1] = pb[half:]
        send1[k] = halves[k, 1 - core].astype(bf16)
        at_once(lambda: first[k].start())

    def join(k):
        first[k].wait_recv()
        both = (halves[k, core] + recv1[k].astype(f32)).reshape(planes, 2, part, width)
        if k:
            send2[k] = both[:, 0].astype(bf16)
            at_once(lambda: second[k].start())
        else:
            total[...] = both[:, 0]
        sendv[:, k] = both[:, 1].astype(bf16)

    form(2)
    form(1)
    loads[0].wait()
    xrows = x_ref.shape[1] // LANES
    for d in range(2):
        for i in range(xrows):
            xe[pl.ds(d * (xrows + lead) + lead + i, 1), :] = x_ref[
                d : d + 1, i * LANES : (i + 1) * LANES
            ]
    edges = [
        remote(
            xe.at[pl.ds(d * (xrows + lead) + xrows, lead), :], edge.at[d], 4, bins + d, following
        )
        for d in range(2)
    ]
    at_once(lambda: [e.start() for e in edges])
    join(2)
    form(3)
    join(1)
    form(0)
    join(3)
    join(0)

    @pl.loop(1, planes, unroll=True)
    def _(k):
        spread(k).start()

    for d in range(2):
        edges[d].wait_recv()
        xe[pl.ds(d * (xrows + lead), lead), :] = jnp.where(at > 0, edge[d], 0.0)
    decimate(rvs, xe[...])
    for entry in plan[:1]:
        build_strip(entry, rvs[entry[0]], strip)

    for k in range(1, bins):
        second[k].wait_recv()
        total[...] = total[...] + recv2[k].astype(f32)
    send3[...] = total[...].astype(bf16)

    @pl.loop(1, planes, unroll=True)
    def _(k):
        third(k).start()

    @pl.loop(1, planes, unroll=True)
    def _(k):
        spread(k).wait_recv()

    acc = sendv[place].astype(f32)
    for k in range(1, planes):
        acc = acc + recvv[k].astype(f32)
    for k in range(1, bins):
        sendy[k] = acc[k].astype(bf16)
        at_once(lambda: across[k].start())

    for entry in plan[1:2]:
        build_strip(entry, rvs[entry[0]], strip)

    @pl.loop(1, planes, unroll=True)
    def _(k):
        third(k).wait_recv()

    one = total[place]
    for k in range(1, planes):
        one = one + recv3[k].astype(f32)
    two = acc[0]
    for k in range(1, bins):
        across[k].wait_recv()
        two = two + recvy[k].astype(f32)
    full[core, place] = jnp.concatenate([one, two], axis=0)
    hand(0).start()

    @pl.loop(1, planes, unroll=True)
    def _(k):
        fourth(k).start()

    for entry in plan[2:]:
        build_strip(entry, rvs[entry[0]], strip)

    @pl.loop(1, planes, unroll=True)
    def _(k):
        fourth(k).wait_recv()
        hand(k).start()

    for d in range(2):
        edges[d].wait_send()
    for k in range(bins):
        first[k].wait_send()
    for k in range(1, bins):
        second[k].wait_send()
        across[k].wait_send()

    @pl.loop(1, planes, unroll=True)
    def _(k):
        spread(k).wait_send()
        third(k).wait_send()
        fourth(k).wait_send()

    @pl.loop(0, planes, unroll=True)
    def _(k):
        hand(k).wait()

    product_ref[...] = full[...].reshape(length, width)


def products(bins, group_size, lead, plan, held, templates, owner, rate, gains, sketch, strain):
    rows, length = templates.shape
    width = sketch.shape[1]
    levels = gains.shape[0]
    planes = group_size // 2
    half, part = length // 2, length // group_size // 2
    hbm = lambda: pl.BlockSpec(memory_space=pltpu.HBM)
    xrows = strain.shape[1] // LANES + lead
    vm = lambda: pl.BlockSpec(memory_space=pltpu.VMEM)
    far = lambda a: pltpu.with_memory_space_constraint(a, pltpu.HBM)
    return pl.pallas_call(
        functools.partial(product_kernel, bins, group_size, planes, lead, plan, levels),
        out_shape=[
            jax.ShapeDtypeStruct((rows, length), bf16),
            jax.ShapeDtypeStruct((length, width), f32),
            jax.ShapeDtypeStruct((LANES, held * LANES), bf16),
            jax.ShapeDtypeStruct((1, rows), jnp.int32),
        ],
        in_specs=[hbm() for _ in range(6)],
        out_specs=[vm() for _ in range(4)],
        scratch_shapes=[
            pltpu.VMEM(templates.shape, bf16),
            pltpu.VMEM(owner.shape, jnp.int32),
            pltpu.VMEM(rate.shape, jnp.int32),
            pltpu.VMEM(gains.shape, f32),
            pltpu.VMEM(sketch.shape, f32),
            pltpu.VMEM(strain.shape, f32),
            pltpu.VMEM((length, rows), bf16),
            pltpu.VMEM((bins, 2, half, width), f32),
            pltpu.VMEM((bins, half, width), bf16),
            pltpu.VMEM((bins, half, width), bf16),
            pltpu.VMEM((bins, planes, part, width), bf16),
            pltpu.VMEM((bins, planes, part, width), bf16),
            pltpu.VMEM((planes, bins, part, width), bf16),
            pltpu.VMEM((planes, bins, part, width), bf16),
            pltpu.VMEM((planes, part, width), f32),
            pltpu.VMEM((planes, part, width), bf16),
            pltpu.VMEM((planes, part, width), bf16),
            pltpu.VMEM((bins, part, width), bf16),
            pltpu.VMEM((bins, part, width), bf16),
            pltpu.VMEM((2, planes, 2 * part, width), f32),
            pltpu.VMEM((2, lead, LANES), f32),
            pltpu.VMEM((2 * xrows, LANES), f32),
        ]
        + [pltpu.VMEM((2 * xrows >> r, LANES), f32) for r in range(levels)]
        + [pltpu.SemaphoreType.DMA((6,)), pltpu.SemaphoreType.DMA((7, 2, planes))],
        compiler_params=pltpu.CompilerParams(
            vmem_limit_bytes=30 << 20, collective_id=0, has_side_effects=True
        ),
        name="products",
    )(far(templates), far(owner), far(rate), far(gains), far(sketch), far(strain))


def eliminate(D, nb):
    w, groups = 8, nb // 8
    ri = lax.broadcasted_iota(jnp.int32, (nb, nb), 0)
    ci = lax.broadcasted_iota(jnp.int32, (nb, nb), 1)
    eye = jnp.where(ri == ci, 1.0, 0.0).astype(f32)
    left = [D[8 * k : 8 * k + 8, :] for k in range(groups)]
    right = [eye[8 * k : 8 * k + 8, :] for k in range(groups)]
    sub = lax.broadcasted_iota(jnp.int32, (8, nb), 0)
    spread = lambda x: jnp.broadcast_to(x, (8, nb))
    for g in range(groups):
        j = g * w
        a = [spread(left[g][s : s + 1, :]) for s in range(w)]
        b = [spread(right[g][s : s + 1, :]) for s in range(w)]
        S = [
            [spread(a[s][:, j + t : j + t + 1]) if t >= s else None for t in range(w)]
            for s in range(w)
        ]
        inv = []
        for s in range(w):
            iv = 1.0 / S[s][s]
            inv.append(iv)
            for t in range(s + 1, w):
                f = S[s][t] * iv
                for u in range(t, w):
                    S[t][u] = S[t][u] - f * S[s][u]
                a[t] = a[t] - f * a[s]
                b[t] = b[t] - f * b[s]
        for k in range(g + 1, groups):
            c = [spread(left[k][:, j + s : j + s + 1]) for s in range(w)]
            lk, rk = left[k], right[k]
            for s in range(w):
                m = c[s] * inv[s]
                lk = lk - m * a[s]
                rk = rk - m * b[s]
                for t in range(s + 1, w):
                    c[t] = c[t] - m * S[s][t]
            left[k], right[k] = lk, rk
        l_own, r_own = a[0], b[0]
        for s in range(1, w):
            l_own = jnp.where(sub == s, a[s], l_own)
            r_own = jnp.where(sub == s, b[s], r_own)
        left[g], right[g] = l_own, r_own
    diag = jnp.where(ri == ci, jnp.concatenate(left, axis=0), 0.0)
    d_col = jnp.sum(diag, axis=1, keepdims=True)
    d_row = jnp.sum(diag, axis=0, keepdims=True)
    return jnp.concatenate(right, axis=0) * lax.rsqrt(d_col), d_row * lax.rsqrt(d_row)


def strip_plan(tiles, length, levels, lead):
    plan, base = [], 0
    for r in range(levels):
        blocks = max(1, (length >> r) // LANES)
        rows = (tiles + lead) >> r
        held = (tiles >> r) + blocks - 1
        chunk = next(m for m in (17, 16, 8, 4, 2, 1) if held % m == 0 or (m == 17 and held > 17 and held % 17 >= 15))
        for d in range(2):
            plan.append((r, d, tiles >> r, blocks, rows, chunk, -(-held // chunk), base))
            base += -(-held // chunk) * chunk
    return plan, base


def decimate(rvs, x):
    n = LANES
    ri = lax.broadcasted_iota(jnp.int32, (n, n), 0)
    ci = lax.broadcasted_iota(jnp.int32, (n, n), 1)
    flip = jnp.where(ri + ci == n - 1, 1.0, 0.0).astype(f32)
    first = jnp.where(ri // 2 == ci, 1.0, 0.0).astype(f32)
    second = jnp.where(ri // 2 == ci - n // 2, 1.0, 0.0).astype(f32)
    rvs[0][...] = dot(x, flip, 1, 0, highest)
    for r in range(1, len(rvs)):
        count = rvs[r].shape[0]
        later = rvs[r - 1][pl.ds(1, count, stride=2), :]
        earlier = rvs[r - 1][pl.ds(0, count, stride=2), :]
        rvs[r][...] = (
            dot(later, first, 1, 0, highest) + dot(earlier, second, 1, 0, highest)
        ) * inv_root_two


def build_strip(entry, rv, strip):
    r, d, tiles, blocks, rows, chunk, count, base = entry
    n = LANES
    wide = chunk + 1
    span = (wide + 1) * n

    def step(i, carry):
        q = d * rows + rows - 1 - i * chunk
        z = jnp.concatenate(
            [rv[pl.ds(jnp.maximum(q - j, 0), 1), :] for j in range(wide + 1)], axis=1
        ).astype(bf16).astype(f32)
        z = jnp.broadcast_to(z, (16, span))
        z = pltpu.roll(z, span - 15, 1, stride=1, stride_axis=0)[:, : wide * n]
        at = pl.ds(pl.multiple_of((base + i * chunk) * n, n), chunk * n)
        for g in range(n // 16):
            k = n - 16 - 16 * g
            t = pltpu.roll(z, wide * n - k, 1) if k else z
            strip[16 * g : 16 * g + 16, at] = t[:, : chunk * n].astype(bf16)
        return carry

    lax.fori_loop(0, count, step, 0)


def filter_level(entry, strip, weight, group, emit):
    r, d, tiles, blocks, rows, chunk, count, base = entry
    n = LANES
    group = min(group, tiles)
    span = group * n

    def tile(s, carry):
        parts = []
        for t in range(group):
            p = base + tiles - 1 - (s * group + t)
            parts.append(strip[:, pl.ds(pl.multiple_of(p * n, n), blocks * n)])
        at = pl.ds(pl.multiple_of(s * span, span), span)
        emit(at, dot(jnp.concatenate(parts, axis=0), weight, 1, 0).astype(bf16))
        return carry

    lax.fori_loop(0, tiles // group, tile, 0)


def finish_kernel(
    bins, scale, plan, levels, p_ref, white_ref, bin_ref, strip, basis_ref, spec_ref, mix_ref, *rest
):
    small, (A, bases, bwide, sems) = rest[: levels - 1], rest[levels - 1 :]
    length, width = p_ref.shape
    nb = width // 2
    bin_at, at = lax.axis_index("bin"), lax.axis_index("grp")
    mesh_id = pl.DeviceIdType.MESH

    def other(k):
        return ((bin_at + k) & (bins - 1), at)

    core = at & 1
    sibling = (bin_at, at + 1 - 2 * core)
    barrier = pltpu.get_barrier_semaphore()
    for peer in [other(k) for k in range(1, bins)] + [sibling]:
        pl.semaphore_signal(barrier, inc=1, device_id=peer, device_id_type=mesh_id)

    def remote(src, dst, group, h, k, device):
        return pltpu.make_async_remote_copy(
            src_ref=src, dst_ref=dst, send_sem=sems.at[group, 0, h, k],
            recv_sem=sems.at[group, 1, h, k], device_id=device, device_id_type=mesh_id,
        )

    farthest_first = sorted(range(1, bins), key=lambda k: -min(k, bins - k))
    sends = [
        {
            k: remote(bases.at[0, h, core], bases.at[bins - k, h, core], 0, h, k, other(k))
            for k in farthest_first
        }
        for h in range(2)
    ]
    hands = [
        {
            k: remote(bases.at[bins - k, h, core], bases.at[bins - k, h, core], 1, h, k, sibling)
            for k in farthest_first
        }
        for h in range(2)
    ]
    p0 = p_ref[:, :nb]
    A[...] = dot(p_ref[...], p_ref[...], 0, 0, highest)
    x0, d0 = eliminate(A[:nb, :nb], nb)
    q0 = dot(p0, x0, 1, 1, highest)
    basis_ref[:, :nb] = q0.astype(bf16)
    bases[0, 0] = q0.astype(bf16).reshape(2, length // 2, nb)
    pl.semaphore_wait(barrier, bins)
    at_once(lambda: [send.start() for send in sends[0].values()])
    r01 = dot(x0, A[:nb, nb:], 1, 0, highest)
    left = p_ref[:, nb:] - dot(q0, r01, 1, 0, highest)
    x1, d1 = eliminate(A[nb:, nb:] - dot(r01, r01, 0, 0, highest), nb)
    q1 = dot(left, x1, 1, 1, highest)
    basis_ref[:, nb:] = q1.astype(bf16)
    bases[0, 1] = q1.astype(bf16).reshape(2, length // 2, nb)
    at_once(lambda: [send.start() for send in sends[1].values()])
    for k in farthest_first:
        sends[0][k].wait_recv()
    at_once(lambda: [hand.start() for hand in hands[0].values()])
    spec_ref[...] = jnp.concatenate([d0, d1], axis=1) * scale
    n = LANES
    for h in range(bwide.shape[0]):
        bwide[h] = basis_ref[:, h * n : (h + 1) * n].astype(f32)
    for entry in plan[2:]:
        r, d = entry[:2]
        taps = length >> r
        weight = jnp.concatenate(
            [bwide[h, pl.ds(0, taps, stride=1 << r), :] for h in range(bwide.shape[0])], axis=1
        )
        if taps < n:
            weight = jnp.concatenate([weight, jnp.zeros((n - taps, width), f32)], axis=0)

        def emit(where, value, r=r, d=d):
            small[r - 1][d, where, :] = value

        filter_level(entry, strip, weight.astype(bf16), 16, emit)
    white = white_ref[...]
    rows = white.shape[0]
    bin_col = jnp.transpose(jnp.broadcast_to(bin_ref[...], (8, rows)).astype(f32))[:, 0:1]
    acc = dot(white, basis_ref[...], 1, 0)
    for k in reversed(farthest_first):
        sends[1][k].wait_recv()
        at_once(lambda k=k: hands[1][k].start())
    for k in reversed(farthest_first):
        for h in range(2):
            hands[h][k].wait_recv()
        slot = bins - k
        theirs = jnp.concatenate([bases[slot, h].reshape(length, nb) for h in range(2)], axis=1)
        acc = jnp.where(bin_col == float(slot), dot(white, theirs, 1, 0), acc)
    mix_ref[...] = acc.astype(bf16)
    for h in range(2):
        for k in farthest_first:
            sends[h][k].wait_send()
            hands[h][k].wait_send()


def finish(bins, scale, plan, levels, product, white, relative, strip):
    length, width = product.shape
    rows = white.shape[0]
    samples = plan[0][2] * LANES
    vm = lambda: pl.BlockSpec(memory_space=pltpu.VMEM)
    return pl.pallas_call(
        functools.partial(finish_kernel, bins, scale, plan, levels),
        out_shape=[
            jax.ShapeDtypeStruct((length, width), bf16),
            jax.ShapeDtypeStruct((1, width), f32),
            jax.ShapeDtypeStruct((rows, width), bf16),
        ]
        + [jax.ShapeDtypeStruct((2, samples >> r, width), bf16) for r in range(1, levels)],
        in_specs=[vm() for _ in range(4)],
        out_specs=[vm() for _ in range(levels + 2)],
        scratch_shapes=[
            pltpu.VMEM((width, width), f32),
            pltpu.VMEM((bins, 2, 2, length // 2, width // 2), bf16),
            pltpu.VMEM((width // LANES, length, LANES), f32),
            pltpu.SemaphoreType.DMA((2, 2, 2, bins)),
        ],
        compiler_params=pltpu.CompilerParams(
            vmem_limit_bytes=24 << 20, collective_id=1, has_side_effects=True
        ),
        name="finish",
    )(product, white, relative, strip)


def output_kernel(plan, levels, strip, basis_ref, spec_ref, mix_ref, *rest):
    small, outs, held, sems = (
        rest[: levels - 1], rest[levels - 1 : 2 * levels + 1], rest[-2], rest[-1]
    )
    mix_out, spec_out, filtered = outs[0], outs[1], outs[2:]
    stores = [
        pltpu.make_async_copy(src, dst, sems.at[1 + i])
        for i, (src, dst) in enumerate(
            [(small[r - 1], filtered[r].at[0]) for r in range(1, levels)]
            + [(mix_ref, mix_out), (spec_ref, spec_out)]
        )
    ]
    for store in stores:
        store.start()
    weight = basis_ref[...]
    for entry in plan[:2]:
        d = entry[1]

        def emit(where, value, d=d):
            held[d, where, :] = value
            pltpu.make_async_copy(
                held.at[d, where, :], filtered[0].at[0, d, where, :], sems.at[0]
            ).start()

        filter_level(entry, strip, weight, 32, emit)
    pltpu.make_async_copy(held, filtered[0].at[0], sems.at[0]).wait()
    for store in stores:
        store.wait()


def output(plan, levels, strip, basis, spectrum, mixed, small):
    width = basis.shape[1]
    samples = plan[0][2] * LANES
    vm = lambda: pl.BlockSpec(memory_space=pltpu.VMEM)
    return pl.pallas_call(
        functools.partial(output_kernel, plan, levels),
        out_shape=[
            jax.ShapeDtypeStruct(mixed.shape, bf16),
            jax.ShapeDtypeStruct(spectrum.shape, f32),
        ]
        + [jax.ShapeDtypeStruct((1, 2, samples >> r, width), bf16) for r in range(levels)],
        in_specs=[vm() for _ in range(levels + 3)],
        out_specs=[pl.BlockSpec(memory_space=pl.ANY)] * (levels + 2),
        scratch_shapes=[
            pltpu.VMEM((2, samples, width), bf16),
            pltpu.SemaphoreType.DMA((levels + 2,)),
        ],
        compiler_params=pltpu.CompilerParams(vmem_limit_bytes=24 << 20),
        name="output",
    )(strip, basis, spectrum, mixed, *small)


def local(bins, group_size, templates, owner_device, rate_code, rate_gains, sketch, strain):
    rows, length = templates.shape
    levels = rate_gains.shape[0]
    lead = 16
    scale = 1.0 / (rows * group_size * math.sqrt(length))
    plan, held = strip_plan(strain.shape[1] // LANES, length, levels, lead)
    white, product, strip, relative = products(
        bins, group_size, lead, plan, held, templates, owner_device.reshape(1, rows),
        rate_code.reshape(1, rows), rate_gains, sketch, strain,
    )
    basis, spectrum, mixed, *small = finish(
        bins, scale, plan, levels, product, white, relative, strip
    )
    return tuple(output(plan, levels, strip, basis, spectrum, mixed, small))


def solution(mesh):
    return jax.shard_map(
        functools.partial(local, mesh.shape["bin"], mesh.shape["grp"]),
        mesh=mesh,
        in_specs=(
            P(("bin", "grp"), None),
            P(("bin", "grp"), None),
            P(("bin", "grp")),
            P(),
            P(),
            P(None, "grp"),
        ),
        out_specs=(P(("bin", "grp"), None), P("bin", None)) + (P("bin", None, "grp", None),) * 5,
        check_vma=False,
    )
```
